32 devices in a mesh: lat: 8 (over y, x, core), lon: 4 (over z).
Axes of the slice: x: 2, y: 2, z: 4, core: 2. Of those that a mesh axis runs over, the one named last changes fastest.
Arguments:
- tracers: float32 [5, 16, 72, 1440], P(None, None, 'lat', 'lon'), may hold values from -6 to 6
- zonal_wind: float32 [16, 72, 1440], P(None, 'lat', 'lon'), may hold values from -0.45 to 0.45
- meridional_wind: float32 [16, 72, 1440], P(None, 'lat', 'lon'), may hold values from -0.45 to 0.45
- cutoff: int32 [72], P('lat'), may hold values from 1 to 720, as said below
Outputs:
- filtered: float32 [5, 16, 72, 1440], P(None, None, 'lat', 'lon')
The draws below stay inside these ranges and needn't reach their ends.
Inputs may be any that keep to these rules, and one draw needn't show every extreme that they name: cutoff is 720 on every row at least 12 rows from both poles and below it on the rows nearer a pole; it is 1 on row 0 and row 71.
All inputs are finite; a program needn't handle non-finite values.
Results may differ from the reference program's by a relative error of at most 0.000075.
Values sent between devices are 32-bit elements; how exact they have to be, the bound alone decides.
No kernel may reach another device: no remote copies, remote signals or barrier semaphores. Data moves between devices by JAX's collectives and lax.ppermute only.
A program may use at most 64 MiB of HBM per device.

```python
import jax
import jax.numpy as jnp

NLON = 1440
F = 5
LEV = 16
NLAT = 72
POLAR = 12


def draw_cutoff(key, part):
    row_index = jnp.arange(NLAT, dtype=jnp.int32)
    distance = jnp.minimum(row_index, NLAT - 1 - row_index)
    half_lon = NLON // 2
    jitter = jax.random.randint(key, (NLAT,), -4, 5).astype(jnp.int32)
    base_value = distance * (half_lon - 1) // POLAR
    values = jnp.clip(base_value + jitter, 1, half_lon - 1)
    values = jnp.where(distance == 0, 1, values)
    values = jnp.where(distance >= POLAR, half_lon, values)
    return values.astype(jnp.int32)


def level_of(rng, dims, split, least, largest):
    loudness = 1.0
    for dim, shards_of in split:
        steps = jax.random.uniform(jax.random.fold_in(jax.random.fold_in(rng, 6), dim), (shards_of,), jnp.float32, least / len(split), largest / len(split))
        loudness = loudness * jnp.repeat(jnp.exp(steps), dims[dim] // shards_of).reshape((-1,) + (1,) * (len(dims) - 1 - dim))
    return loudness


def normal_values(key, dims, scale, most, cuts=(), kind=jnp.bfloat16):
    factor_of = level_of(key, dims, cuts, -0.22, 0.18) if cuts else 1.0
    values = jax.random.normal(key, dims, jnp.float32) * scale * factor_of
    return jnp.minimum(jnp.maximum(values, -most), most).astype(kind)


def setup_inputs(seed: int = 0) -> dict:
    streams_of = jax.random.split(jax.random.key(seed), 5)
    return {
        "tracers": normal_values(streams_of[0], (F, LEV, NLAT, NLON), 1.0, 6.0, ((2, 8), (3, 4)), jnp.float32),
        "zonal_wind": jnp.clip(jax.random.uniform(streams_of[1], (LEV, NLAT, NLON), jnp.float32, -0.45, 0.45) * level_of(streams_of[1], (LEV, NLAT, NLON), ((1, 8), (2, 4)), -0.4, 0.0), -0.45, 0.45),
        "meridional_wind": jnp.clip(jax.random.uniform(streams_of[2], (LEV, NLAT, NLON), jnp.float32, -0.45, 0.45) * level_of(streams_of[2], (LEV, NLAT, NLON), ((1, 8), (2, 4)), -0.4, 0.0), -0.45, 0.45),
        "cutoff": draw_cutoff(jax.random.fold_in(streams_of[4], 71), 0),
    }


def extend(field, flip):
    half_lon = field.shape[-1] // 2
    north = jnp.roll(field[..., :1, :], half_lon, axis=-1) * flip
    south = jnp.roll(field[..., -1:, :], half_lon, axis=-1) * flip
    padded = jnp.concatenate([north, field, south], axis=-2)
    return jnp.concatenate([padded[..., -1:], padded, padded[..., :1]], axis=-1)


def advect(q_pad, u_pad, v_pad):
    center = q_pad[..., 1:-1, 1:-1]
    u_mid = u_pad[..., 1:-1, 1:-1]
    east_speed = 0.5 * (u_mid + u_pad[..., 1:-1, 2:])
    west_speed = 0.5 * (u_pad[..., 1:-1, :-2] + u_mid)
    east_flux = jnp.maximum(east_speed, 0.0) * center + jnp.minimum(east_speed, 0.0) * q_pad[..., 1:-1, 2:]
    west_flux = jnp.maximum(west_speed, 0.0) * q_pad[..., 1:-1, :-2] + jnp.minimum(west_speed, 0.0) * center
    v_mid = v_pad[..., 1:-1, 1:-1]
    south_speed = 0.5 * (v_mid + v_pad[..., 2:, 1:-1])
    north_speed = 0.5 * (v_pad[..., :-2, 1:-1] + v_mid)
    south_flux = jnp.maximum(south_speed, 0.0) * center + jnp.minimum(south_speed, 0.0) * q_pad[..., 2:, 1:-1]
    north_flux = jnp.maximum(north_speed, 0.0) * q_pad[..., :-2, 1:-1] + jnp.minimum(north_speed, 0.0) * center
    return center - (east_flux - west_flux) - (south_flux - north_flux)


def reference(tracers, zonal_wind, meridional_wind, cutoff):
    stepped = advect(extend(tracers, 1.0), extend(zonal_wind, 1.0), extend(meridional_wind, -1.0))
    spectrum = jnp.fft.rfft(stepped, axis=-1)
    wave_number = jnp.arange(NLON // 2 + 1).astype(jnp.int32)
    keep = wave_number[None, :] <= cutoff.astype(jnp.int32)[:, None]
    spectrum = jnp.where(keep, spectrum, 0.0)
    return jnp.fft.irfft(spectrum, n=NLON, axis=-1).astype(jnp.float32)
```

```python
import math

import jax
import jax.numpy as jnp
from jax import lax
from jax.experimental import pallas as pl
from jax.experimental.pallas import tpu as pltpu
from jax.sharding import PartitionSpec as P

LANES = 128
EDGES = 4


class Plan:
    def __init__(self, fields, levels, rows, sector, n_lat, n_lon):
        self.fields, self.levels, self.rows, self.sector = fields, levels, rows, sector
        self.n_lat, self.n_lon = n_lat, n_lon
        self.planes = fields * levels
        self.circle = sector * n_lon
        self.quarter = self.circle // 4
        cap = rows * n_lat // 6
        self.full = (cap - 1) // rows
        self.n_x = cap - self.full * rows
        self.n_y = rows - self.n_x
        self.width = -(-(sector + EDGES) // LANES) * LANES
        self.x_count = self.n_x * self.planes // n_lon
        self.y_count = self.n_y * self.planes // n_lon
        self.x_full = [0] + list(range(1 + self.n_y, rows))

    def pieces(self, index, count):
        start, out = index * self.planes, []
        stop = start + self.planes
        while start < stop:
            chunk, offset = divmod(start, count)
            size = min(count - offset, stop - start)
            out.append((chunk, offset, start - index * self.planes, size))
            start += size
        return out

    def x_row(self, index, lat):
        full = (lat < self.full) | (lat >= self.n_lat - self.full)
        south = lat >= self.n_lat // 2
        partial = jnp.where(south, self.rows - self.n_x + index, index)
        return jnp.where(full, self.x_full[index], partial)


def split_speed(speed):
    return jnp.maximum(speed, 0.0), jnp.minimum(speed, 0.0)


def tiled(x, fields):
    return jnp.concatenate([x] * fields, axis=0) if fields > 1 else x


def back(x, width):
    return pltpu.roll(x, width - 1, 1)


def inner_rows_kernel(plan, q_ref, u_ref, v_ref, *refs):
    outs, buf, q_pad, u_pad = refs[: plan.n_lon], *refs[plan.n_lon :]
    width, sector = plan.width, plan.sector
    lane = lax.broadcasted_iota(jnp.int32, (plan.levels, width), 1)
    inside = lane < sector - 1
    q_pad[...] = jnp.zeros_like(q_pad)
    u_pad[...] = jnp.zeros_like(u_pad)
    wide = lax.broadcasted_iota(jnp.int32, (plan.planes, width), 1)

    def south_flux(r):
        plus, minus = split_speed(0.5 * (v_ref[r] + v_ref[r + 1]))
        return tiled(plus, plan.fields) * q_ref[r] + tiled(minus, plan.fields) * q_ref[r + 1]

    north = south_flux(0)
    for i in range(plan.n_y):
        r = 1 + i
        q_pad[:, 0:sector] = q_ref[r]
        u_pad[:, 0:sector] = u_ref[r]
        q, u = q_pad[...], u_pad[...]
        plus, minus = split_speed(0.5 * (u + back(u, width)))
        plus, minus = jnp.where(inside, plus, 0.0), jnp.where(inside, minus, 0.0)
        east = tiled(plus, plan.fields) * q + tiled(minus, plan.fields) * back(q, width)
        stepped = q - (east - pltpu.roll(east, 1, 1))
        south = south_flux(r)
        first_u, last_u = tiled(u[:, 0:1], plan.fields), tiled(u[:, sector - 1 : sector], plan.fields)
        stepped = jnp.where(wide == sector, q[:, 0:1], stepped)
        stepped = jnp.where(wide == sector + 1, q[:, sector - 1 : sector], stepped)
        stepped = jnp.where(wide == sector + 2, first_u, stepped)
        stepped = jnp.where(wide == sector + 3, last_u, stepped)
        q_pad[...] = stepped
        q_pad[:, 0:sector] = q_pad[:, 0:sector] - (south - north)
        for chunk, offset, first, size in plan.pieces(i, plan.y_count):
            buf[chunk, offset : offset + size, :] = q_pad[first : first + size, :]
        north = south
    lon = lax.axis_index("lon")
    for s in range(plan.n_lon):
        outs[s][...] = buf[lax.rem(lon + s, plan.n_lon)]


def all_rows_kernel(plan, q_ref, u_ref, v_ref, one_ref, two_ref, west_ref, east_ref, *refs):
    outs, done, buf, q_pad, u_pad, stage = refs[: plan.n_lon], *refs[plan.n_lon :]
    width, sector, planes, rows = plan.width, plan.sector, plan.planes, plan.rows
    lat = lax.axis_index("lat")
    odd = lax.rem(lat, 2) == 1
    sign_north = jnp.where(lat == 0, -1.0, 1.0)
    sign_south = jnp.where(lat == plan.n_lat - 1, -1.0, 1.0)
    one, two = one_ref[...], two_ref[...]
    above, below = jnp.where(odd, two, one), jnp.where(odd, one, two)
    q_above, v_above = above[:planes], above[planes:] * sign_north
    q_below, v_below = below[:planes], below[planes:] * sign_south
    q_pad[...] = jnp.zeros_like(q_pad)
    u_pad[...] = jnp.zeros_like(u_pad)

    def face(v_low, v_high, q_low, q_high):
        plus, minus = split_speed(0.5 * (v_low + v_high))
        return tiled(plus, plan.fields) * q_low + tiled(minus, plan.fields) * q_high

    north = face(v_above, v_ref[0], q_above, q_ref[0])
    for r in range(rows):
        q_pad[:, 0:sector] = q_ref[r]
        u_pad[:, 0:sector] = u_ref[r]
        q_pad[:, sector : sector + 1] = east_ref[:planes, r : r + 1]
        u_pad[:, sector : sector + 1] = east_ref[planes:, r : r + 1]
        q_pad[:, width - 1 : width] = west_ref[:planes, r : r + 1]
        u_pad[:, width - 1 : width] = west_ref[planes:, r : r + 1]
        q, u = q_pad[...], u_pad[...]
        plus, minus = split_speed(0.5 * (u + back(u, width)))
        east = tiled(plus, plan.fields) * q + tiled(minus, plan.fields) * back(q, width)
        stage[r] = q - (east - pltpu.roll(east, 1, 1))
        if r + 1 < rows:
            south = face(v_ref[r], v_ref[r + 1], q_ref[r], q_ref[r + 1])
        else:
            south = face(v_ref[r], v_below, q_ref[r], q_below)
        value = stage[r, :, 0:sector] - (south - north)
        stage[r, :, 0:sector] = value
        done[r] = value
        north = south
    for j in range(plan.n_x):
        r = plan.x_row(j, lat)
        for chunk, offset, first, size in plan.pieces(j, plan.x_count):
            buf[chunk, offset : offset + size, :] = stage[r, first : first + size, :]
    lon = lax.axis_index("lon")
    for s in range(plan.n_lon):
        outs[s][...] = buf[lax.rem(lon + s, plan.n_lon)]


def product(x, table_hi, table_lo, transposed):
    dims = (((1,), (1 if transposed else 0,)), ((), ()))
    x_hi = x.astype(jnp.bfloat16)
    x_lo = (x - x_hi.astype(jnp.float32)).astype(jnp.bfloat16)
    count = x.shape[0]
    both = lax.dot_general(
        jnp.concatenate([x_hi, x_lo], axis=0), table_hi, dims, preferred_element_type=jnp.float32
    )
    low = lax.dot_general(x_hi, table_lo, dims, preferred_element_type=jnp.float32)
    return both[:count] + both[count:] + low


def filter_quarters(plan, quarters, cut, hi, lo):
    x0, x1, x2, x3 = quarters
    a, b, u, v = x0 + x2, x1 + x3, x0 - x2, x1 - x3
    count, size, circle = x0.shape[0], plan.quarter, plan.circle
    m = lax.broadcasted_iota(jnp.int32, (count, size), 1)

    def kept(h, r):
        k = 4 * m + r
        return jnp.where(jnp.minimum(k, circle - k) <= cut, h, 0.0) * (1.0 / circle)

    def times(x, i, transposed=False):
        return product(x, hi[i], lo[i], transposed)

    h0 = kept(times(a + b, 0), 0)
    h2 = kept(times(a - b, 1), 2)
    h1 = kept(times(u, 2) + times(v, 4), 1)
    h3 = kept(times(u, 3) + times(v, 5), 3)
    even, twice = times(h0, 0, True), times(h2, 1, True)
    o_u = times(h1, 2, True) + times(h3, 3, True)
    o_v = times(h1, 4, True) + times(h3, 5, True)
    both, apart = even + twice, even - twice
    return both + o_u, apart + o_v, both - o_u, apart - o_v


def filter_kernel(plan, count, row_of, with_edges, cut_ref, hi_ref, lo_ref, *refs):
    n = plan.n_lon
    ins, outs = refs[:n], refs[n : 2 * n]
    sector = plan.sector
    lat, lon = lax.axis_index("lat"), lax.axis_index("lon")
    circle_index = lon * count + lax.broadcasted_iota(jnp.int32, (count, 1), 0)
    cut = jnp.full((count, 1), plan.circle, jnp.int32)
    rows_here = (plan.n_y if with_edges else plan.n_x)
    for i in range(rows_here):
        here = (circle_index >= i * plan.planes) & (circle_index < (i + 1) * plan.planes)
        cut = jnp.where(here, cut_ref[row_of(i, lat)], cut)
    pieces = [ref[:, 0:sector] for ref in ins]
    if with_edges:
        tails = [ref[:, sector : sector + EDGES] for ref in ins]
        lane = lax.broadcasted_iota(jnp.int32, (count, sector), 1)
        fluxes = []
        for j in range(n):
            here, there = tails[j], tails[(j + 1) % n]
            plus, minus = split_speed(0.5 * (here[:, 3:4] + there[:, 2:3]))
            fluxes.append(plus * here[:, 1:2] + minus * there[:, 0:1])
        pieces = [
            piece - jnp.where(lane == sector - 1, fluxes[j], 0.0) + jnp.where(lane == 0, fluxes[j - 1], 0.0)
            for j, piece in enumerate(pieces)
        ]
    per = n // 4
    quarters = [
        jnp.concatenate(pieces[per * i : per * (i + 1)], axis=1) if per > 1 else pieces[i] for i in range(4)
    ]
    filtered = filter_quarters(plan, quarters, cut, hi_ref, lo_ref)
    for j in range(n):
        part = j % per
        outs[j][...] = filtered[j // per][:, part * sector : (part + 1) * sector]


def merge_kernel(plan, stepped_ref, *refs):
    n = plan.n_lon
    y_ins, x_ins, out, buf = refs[:n], refs[n : 2 * n], refs[2 * n], refs[2 * n + 1]
    lat, lon = lax.axis_index("lat"), lax.axis_index("lon")
    full = (lat < plan.full) | (lat >= plan.n_lat - plan.full)
    part = (lat == plan.full) | (lat == plan.n_lat - 1 - plan.full)

    @pl.when(jnp.logical_not(full))
    def _():
        out[...] = stepped_ref[...]

    @pl.when(full)
    def _():
        for j in range(n):
            buf[lax.rem(lon + n - j, n), 0 : plan.y_count, :] = y_ins[j][...]
        for i in range(plan.n_y):
            for chunk, offset, first, size in plan.pieces(i, plan.y_count):
                out[1 + i, first : first + size, :] = buf[chunk, offset : offset + size, :]

    @pl.when(full | part)
    def _():
        for j in range(n):
            buf[lax.rem(lon + n - j, n), 0 : plan.x_count, :] = x_ins[j][...]
        for i in range(plan.n_x):
            r = plan.x_row(i, lat)
            for chunk, offset, first, size in plan.pieces(i, plan.x_count):
                out[r, first : first + size, :] = buf[chunk, offset : offset + size, :]


def call(kernel, outs, scratch=(), **options):
    return pl.pallas_call(
        kernel,
        out_shape=[jax.ShapeDtypeStruct(shape, jnp.float32) for shape in outs],
        **options,
        scratch_shapes=[pltpu.VMEM(shape, jnp.float32) for shape in scratch],
    )


def transform_tables(plan):
    size, circle = plan.quarter, plan.circle
    inner = max(d for d in range(8, 41, 8) if size % d == 0)
    outer = size // inner
    m = 4 * jnp.arange(size, dtype=jnp.int32)
    k = jnp.stack([m, m + 2, m + 1, m + 3, -(m + 1), -(m + 3)])
    sign = jnp.array([1.0, 1.0, 1.0, 1.0, 1.0, -1.0], jnp.float32)[:, None, None, None]

    def angle(count, step):
        n = step * jnp.arange(count, dtype=jnp.int32)
        return jnp.mod(k[:, None, :] * n[None, :, None], circle).astype(jnp.float32) * (2.0 * math.pi / circle)

    coarse, fine = angle(outer, inner), angle(inner, 1)
    cos_c, sin_c = jnp.cos(coarse)[:, :, None, :], jnp.sin(coarse)[:, :, None, :]
    cos_f, sin_f = jnp.cos(fine)[:, None, :, :], jnp.sin(fine)[:, None, :, :]
    table = sign * (cos_c * (cos_f + sin_f) + sin_c * (cos_f - sin_f))
    table = table.reshape(6, size, size)
    high = lax.reduce_precision(table, 8, 7)
    return high.astype(jnp.bfloat16), (table - high).astype(jnp.bfloat16)


def body(tracers, zonal_wind, meridional_wind, cutoff):
    fields, levels, rows, sector = tracers.shape
    n_lat, n_lon = lax.axis_size("lat"), lax.axis_size("lon")
    plan = Plan(fields, levels, rows, sector, n_lat, n_lon)
    planes, width = plan.planes, plan.width
    q = tracers.reshape(planes, rows, sector)
    u, v = zonal_wind, meridional_wind
    lat_index = lax.axis_index("lat")
    both = ("lat", "lon")

    def device(lat, lon):
        return lat * n_lon + lon % n_lon

    def shift_pairs(lats, by):
        return [(device(a, z), device(a, z + by)) for a in lats for z in range(n_lon)]

    full_lats = list(range(plan.full)) + list(range(n_lat - plan.full, n_lat))
    polar_lats = list(range(plan.full + 1)) + list(range(n_lat - plan.full - 1, n_lat))

    qt, ut, vt = (jnp.transpose(x, (1, 0, 2)) for x in (q, u, v))

    odd = lax.rem(lat_index, 2)
    qv = jnp.concatenate([qt[0], vt[0]], axis=0), jnp.concatenate([qt[-1], vt[-1]], axis=0)
    toward_one = jnp.where(odd == 1, qv[1], qv[0])
    toward_two = jnp.where(odd == 1, qv[0], qv[1])
    pairs_one = shift_pairs((0, n_lat - 1), n_lon // 2)
    for a in range(1, n_lat - 1, 2):
        for z in range(n_lon):
            pairs_one += [(device(a, z), device(a + 1, z)), (device(a + 1, z), device(a, z))]
    pairs_two = [(device(a, z), device(a ^ 1, z)) for a in range(n_lat) for z in range(n_lon)]
    two = lax.ppermute(toward_two, both, pairs_two)
    one = lax.ppermute(toward_one, both, pairs_one)

    y_send = call(
        lambda *refs: inner_rows_kernel(plan, *refs),
        [(plan.y_count, width)] * n_lon,
        [(n_lon, plan.y_count, width), (planes, width), (levels, width)],
    )(qt, ut, vt)
    y_got = [y_send[0]] + [
        lax.ppermute(y_send[s], both, shift_pairs(full_lats, s)) for s in range(1, n_lon)
    ]

    last = jnp.concatenate([q[:, :, -1], u[:, :, -1]], axis=0)
    first = jnp.concatenate([q[:, :, 0], u[:, :, 0]], axis=0)
    west = lax.ppermute(last, "lon", [(i, (i + 1) % n_lon) for i in range(n_lon)])
    east = lax.ppermute(first, "lon", [(i, (i - 1) % n_lon) for i in range(n_lon)])

    *x_send, stepped = call(
        lambda *refs: all_rows_kernel(plan, *refs),
        [(plan.x_count, width)] * n_lon + [(rows, planes, sector)],
        [(n_lon, plan.x_count, width), (planes, width), (levels, width), (rows, planes, width)],
    )(qt, ut, vt, one, two, west, east)
    x_got = [x_send[0]] + [
        lax.ppermute(x_send[s], both, shift_pairs(polar_lats, s)) for s in range(1, n_lon)
    ]

    hi, lo = transform_tables(plan)
    vmem = pl.BlockSpec(memory_space=pltpu.VMEM)
    smem = pl.BlockSpec(memory_space=pltpu.SMEM)

    def filtered(got, count, row_of, with_edges, lats):
        ordered = [got[(n_lon - j) % n_lon] for j in range(n_lon)]
        pieces = call(
            lambda *refs: filter_kernel(plan, count, row_of, with_edges, *refs),
            [(count, sector)] * n_lon,
            in_specs=[smem] + [vmem] * (2 + n_lon),
        )(cutoff, hi, lo, *ordered)
        return [pieces[0]] + [
            lax.ppermute(pieces[s], both, shift_pairs(lats, s)) for s in range(1, n_lon)
        ]

    y_back = filtered(y_got, plan.y_count, lambda i, lat: 1 + i, True, full_lats)
    x_back = filtered(x_got, plan.x_count, plan.x_row, False, polar_lats)
    (merged,) = call(
        lambda *refs: merge_kernel(plan, *refs),
        [(rows, planes, sector)],
        [(n_lon, max(plan.y_count, plan.x_count), sector)],
    )(stepped, *y_back, *x_back)
    return jnp.transpose(merged, (1, 0, 2)).reshape(fields, levels, rows, sector)


def solution(mesh):
    in_specs = (P(None, None, "lat", "lon"), P(None, "lat", "lon"), P(None, "lat", "lon"), P("lat"))
    out_specs = P(None, None, "lat", "lon")
    return jax.shard_map(body, mesh=mesh, in_specs=in_specs, out_specs=out_specs, check_vma=False)
```

```python
import math

import jax
import jax.numpy as jnp
from jax import lax
from jax.experimental import pallas as pl
from jax.experimental.pallas import tpu as pltpu
from jax.sharding import PartitionSpec as P

LANES = 128
EDGES = 4


class Plan:
    def __init__(self, fields, levels, rows, sector, n_lat, n_lon):
        self.fields, self.levels, self.rows, self.sector = fields, levels, rows, sector
        self.n_lat, self.n_lon = n_lat, n_lon
        self.planes = fields * levels
        self.circle = sector * n_lon
        self.quarter = self.circle // 4
        cap = rows * n_lat // 6
        self.full = (cap - 1) // rows
        self.n_x = cap - self.full * rows
        self.n_y = rows - self.n_x
        self.width = -(-(sector + EDGES) // LANES) * LANES
        self.x_count = self.n_x * self.planes // n_lon
        self.y_count = self.n_y * self.planes // n_lon
        self.x_full = [0] + list(range(1 + self.n_y, rows))

    def pieces(self, index, count):
        start, out = index * self.planes, []
        stop = start + self.planes
        while start < stop:
            chunk, offset = divmod(start, count)
            size = min(count - offset, stop - start)
            out.append((chunk, offset, start - index * self.planes, size))
            start += size
        return out

    def x_row(self, index, lat):
        full = (lat < self.full) | (lat >= self.n_lat - self.full)
        south = lat >= self.n_lat // 2
        partial = jnp.where(south, self.rows - self.n_x + index, index)
        return jnp.where(full, self.x_full[index], partial)


def split_speed(speed):
    return jnp.maximum(speed, 0.0), jnp.minimum(speed, 0.0)


def tiled(x, fields):
    return jnp.concatenate([x] * fields, axis=0) if fields > 1 else x


def back(x, width):
    return pltpu.roll(x, width - 1, 1)


def inner_rows_kernel(plan, q_ref, u_ref, v_ref, *refs):
    outs, buf, q_pad, u_pad = refs[: plan.n_lon], *refs[plan.n_lon :]
    width, sector = plan.width, plan.sector
    lane = lax.broadcasted_iota(jnp.int32, (plan.levels, width), 1)
    inside = lane < sector - 1
    q_pad[...] = jnp.zeros_like(q_pad)
    u_pad[...] = jnp.zeros_like(u_pad)
    wide = lax.broadcasted_iota(jnp.int32, (plan.planes, width), 1)

    def south_flux(r):
        plus, minus = split_speed(0.5 * (v_ref[r] + v_ref[r + 1]))
        return tiled(plus, plan.fields) * q_ref[r] + tiled(minus, plan.fields) * q_ref[r + 1]

    north = south_flux(0)
    for i in range(plan.n_y):
        r = 1 + i
        q_pad[:, 0:sector] = q_ref[r]
        u_pad[:, 0:sector] = u_ref[r]
        q, u = q_pad[...], u_pad[...]
        plus, minus = split_speed(0.5 * (u + back(u, width)))
        plus, minus = jnp.where(inside, plus, 0.0), jnp.where(inside, minus, 0.0)
        east = tiled(plus, plan.fields) * q + tiled(minus, plan.fields) * back(q, width)
        stepped = q - (east - pltpu.roll(east, 1, 1))
        south = south_flux(r)
        first_u, last_u = tiled(u[:, 0:1], plan.fields), tiled(u[:, sector - 1 : sector], plan.fields)
        stepped = jnp.where(wide == sector, q[:, 0:1], stepped)
        stepped = jnp.where(wide == sector + 1, q[:, sector - 1 : sector], stepped)
        stepped = jnp.where(wide == sector + 2, first_u, stepped)
        stepped = jnp.where(wide == sector + 3, last_u, stepped)
        q_pad[...] = stepped
        q_pad[:, 0:sector] = q_pad[:, 0:sector] - (south - north)
        for chunk, offset, first, size in plan.pieces(i, plan.y_count):
            buf[chunk, offset : offset + size, :] = q_pad[first : first + size, :]
        north = south
    lon = lax.axis_index("lon")
    for s in range(plan.n_lon):
        outs[s][...] = buf[lax.rem(lon + s, plan.n_lon)]


def all_rows_kernel(plan, q_ref, u_ref, v_ref, one_ref, two_ref, west_ref, east_ref, *refs):
    outs, done, buf, q_pad, u_pad, stage = refs[: plan.n_lon], *refs[plan.n_lon :]
    width, sector, planes, rows = plan.width, plan.sector, plan.planes, plan.rows
    lat = lax.axis_index("lat")
    odd = lax.rem(lat, 2) == 1
    sign_north = jnp.where(lat == 0, -1.0, 1.0)
    sign_south = jnp.where(lat == plan.n_lat - 1, -1.0, 1.0)
    one, two = one_ref[...], two_ref[...]
    above, below = jnp.where(odd, two, one), jnp.where(odd, one, two)
    q_above, v_above = above[:planes], above[planes:] * sign_north
    q_below, v_below = below[:planes], below[planes:] * sign_south
    q_pad[...] = jnp.zeros_like(q_pad)
    u_pad[...] = jnp.zeros_like(u_pad)

    def face(v_low, v_high, q_low, q_high):
        plus, minus = split_speed(0.5 * (v_low + v_high))
        return tiled(plus, plan.fields) * q_low + tiled(minus, plan.fields) * q_high

    north = face(v_above, v_ref[0], q_above, q_ref[0])
    for r in range(rows):
        q_pad[:, 0:sector] = q_ref[r]
        u_pad[:, 0:sector] = u_ref[r]
        q_pad[:, sector : sector + 1] = east_ref[:planes, r : r + 1]
        u_pad[:, sector : sector + 1] = east_ref[planes:, r : r + 1]
        q_pad[:, width - 1 : width] = west_ref[:planes, r : r + 1]
        u_pad[:, width - 1 : width] = west_ref[planes:, r : r + 1]
        q, u = q_pad[...], u_pad[...]
        plus, minus = split_speed(0.5 * (u + back(u, width)))
        east = tiled(plus, plan.fields) * q + tiled(minus, plan.fields) * back(q, width)
        stage[r] = q - (east - pltpu.roll(east, 1, 1))
        if r + 1 < rows:
            south = face(v_ref[r], v_ref[r + 1], q_ref[r], q_ref[r + 1])
        else:
            south = face(v_ref[r], v_below, q_ref[r], q_below)
        value = stage[r, :, 0:sector] - (south - north)
        stage[r, :, 0:sector] = value
        done[r] = value
        north = south
    for j in range(plan.n_x):
        r = plan.x_row(j, lat)
        for chunk, offset, first, size in plan.pieces(j, plan.x_count):
            buf[chunk, offset : offset + size, :] = stage[r, first : first + size, :]
    lon = lax.axis_index("lon")
    for s in range(plan.n_lon):
        outs[s][...] = buf[lax.rem(lon + s, plan.n_lon)]


def product(x, table_hi, table_lo, transposed):
    dims = (((1,), (1 if transposed else 0,)), ((), ()))
    x_hi = x.astype(jnp.bfloat16)
    x_lo = (x - x_hi.astype(jnp.float32)).astype(jnp.bfloat16)
    count = x.shape[0]
    both = lax.dot_general(
        jnp.concatenate([x_hi, x_lo], axis=0), table_hi, dims, preferred_element_type=jnp.float32
    )
    low = lax.dot_general(x_hi, table_lo, dims, preferred_element_type=jnp.float32)
    return both[:count] + both[count:] + low


def filter_quarters(plan, quarters, cut, hi, lo):
    x0, x1, x2, x3 = quarters
    a, b, u, v = x0 + x2, x1 + x3, x0 - x2, x1 - x3
    count, size, circle = x0.shape[0], plan.quarter, plan.circle
    m = lax.broadcasted_iota(jnp.int32, (count, size), 1)

    def kept(h, r):
        k = 4 * m + r
        return jnp.where(jnp.minimum(k, circle - k) <= cut, h, 0.0) * (1.0 / circle)

    def times(x, i, transposed=False):
        return product(x, hi[i], lo[i], transposed)

    h0 = kept(times(a + b, 0), 0)
    h2 = kept(times(a - b, 1), 2)
    h1 = kept(times(u, 2) + times(v, 4), 1)
    h3 = kept(times(u, 3) + times(v, 5), 3)
    even, twice = times(h0, 0, True), times(h2, 1, True)
    o_u = times(h1, 2, True) + times(h3, 3, True)
    o_v = times(h1, 4, True) + times(h3, 5, True)
    both, apart = even + twice, even - twice
    return both + o_u, apart + o_v, both - o_u, apart - o_v


def filter_kernel(plan, count, row_of, with_edges, cut_ref, hi_ref, lo_ref, *refs):
    n = plan.n_lon
    ins, outs = refs[:n], refs[n : 2 * n]
    sector = plan.sector
    lat, lon = lax.axis_index("lat"), lax.axis_index("lon")
    circle_index = lon * count + lax.broadcasted_iota(jnp.int32, (count, 1), 0)
    cut = jnp.full((count, 1), plan.circle, jnp.int32)
    rows_here = (plan.n_y if with_edges else plan.n_x)
    for i in range(rows_here):
        here = (circle_index >= i * plan.planes) & (circle_index < (i + 1) * plan.planes)
        cut = jnp.where(here, cut_ref[row_of(i, lat)], cut)
    pieces = [ref[:, 0:sector] for ref in ins]
    if with_edges:
        tails = [ref[:, sector : sector + EDGES] for ref in ins]
        lane = lax.broadcasted_iota(jnp.int32, (count, sector), 1)
        fluxes = []
        for j in range(n):
            here, there = tails[j], tails[(j + 1) % n]
            plus, minus = split_speed(0.5 * (here[:, 3:4] + there[:, 2:3]))
            fluxes.append(plus * here[:, 1:2] + minus * there[:, 0:1])
        pieces = [
            piece - jnp.where(lane == sector - 1, fluxes[j], 0.0) + jnp.where(lane == 0, fluxes[j - 1], 0.0)
            for j, piece in enumerate(pieces)
        ]
    per = n // 4
    quarters = [
        jnp.concatenate(pieces[per * i : per * (i + 1)], axis=1) if per > 1 else pieces[i] for i in range(4)
    ]
    filtered = filter_quarters(plan, quarters, cut, hi_ref, lo_ref)
    for j in range(n):
        part = j % per
        outs[j][...] = filtered[j // per][:, part * sector : (part + 1) * sector]


def merge_kernel(plan, stepped_ref, *refs):
    n = plan.n_lon
    y_ins, x_ins, out, buf = refs[:n], refs[n : 2 * n], refs[2 * n], refs[2 * n + 1]
    lat, lon = lax.axis_index("lat"), lax.axis_index("lon")
    full = (lat < plan.full) | (lat >= plan.n_lat - plan.full)
    part = (lat == plan.full) | (lat == plan.n_lat - 1 - plan.full)

    @pl.when(jnp.logical_not(full))
    def _():
        out[...] = stepped_ref[...]

    @pl.when(full)
    def _():
        for j in range(n):
            buf[lax.rem(lon + n - j, n), 0 : plan.y_count, :] = y_ins[j][...]
        for i in range(plan.n_y):
            for chunk, offset, first, size in plan.pieces(i, plan.y_count):
                out[1 + i, first : first + size, :] = buf[chunk, offset : offset + size, :]

    @pl.when(full | part)
    def _():
        for j in range(n):
            buf[lax.rem(lon + n - j, n), 0 : plan.x_count, :] = x_ins[j][...]
        for i in range(plan.n_x):
            r = plan.x_row(i, lat)
            for chunk, offset, first, size in plan.pieces(i, plan.x_count):
                out[r, first : first + size, :] = buf[chunk, offset : offset + size, :]


def call(kernel, outs, scratch=(), **options):
    return pl.pallas_call(
        kernel,
        out_shape=[jax.ShapeDtypeStruct(shape, jnp.float32) for shape in outs],
        **options,
        scratch_shapes=[pltpu.VMEM(shape, jnp.float32) for shape in scratch],
    )


def transform_tables(plan):
    size, circle = plan.quarter, plan.circle
    inner = max(d for d in range(8, 41, 8) if size % d == 0)
    outer = size // inner
    m = 4 * jnp.arange(size, dtype=jnp.int32)
    k = jnp.stack([m, m + 2, m + 1, m + 3, -(m + 1), -(m + 3)])
    sign = jnp.array([1.0, 1.0, 1.0, 1.0, 1.0, -1.0], jnp.float32)[:, None, None, None]

    def angle(count, step):
        n = step * jnp.arange(count, dtype=jnp.int32)
        return jnp.mod(k[:, None, :] * n[None, :, None], circle).astype(jnp.float32) * (2.0 * math.pi / circle)

    coarse, fine = angle(outer, inner), angle(inner, 1)
    cos_c, sin_c = jnp.cos(coarse)[:, :, None, :], jnp.sin(coarse)[:, :, None, :]
    cos_f, sin_f = jnp.cos(fine)[:, None, :, :], jnp.sin(fine)[:, None, :, :]
    table = sign * (cos_c * (cos_f + sin_f) + sin_c * (cos_f - sin_f))
    table = table.reshape(6, size, size)
    high = lax.reduce_precision(table, 8, 7)
    return high.astype(jnp.bfloat16), (table - high).astype(jnp.bfloat16)


def body(tracers, zonal_wind, meridional_wind, cutoff):
    fields, levels, rows, sector = tracers.shape
    n_lat, n_lon = lax.axis_size("lat"), lax.axis_size("lon")
    plan = Plan(fields, levels, rows, sector, n_lat, n_lon)
    planes, width = plan.planes, plan.width
    q = tracers.reshape(planes, rows, sector)
    u, v = zonal_wind, meridional_wind
    lat_index = lax.axis_index("lat")
    both = ("lat", "lon")

    def device(lat, lon):
        return lat * n_lon + lon % n_lon

    def shift_pairs(lats, by):
        return [(device(a, z), device(a, z + by)) for a in lats for z in range(n_lon)]

    def x_pairs(by):
        return shift_pairs(range(n_lat), by)

    def y_pairs(by):
        spare = list(range(plan.full + 1, n_lat - plan.full - 1))
        swaps = [(plan.full, n_lat - 1 - plan.full)] + list(zip(spare[0::2], spare[1::2]))
        pairs = shift_pairs(list(range(plan.full)) + list(range(n_lat - plan.full, n_lat)), by)
        for a, b in swaps:
            pairs += [(device(p, z), device(q, z)) for p, q in ((a, b), (b, a)) for z in range(n_lon)]
        return pairs

    qt, ut, vt = (jnp.transpose(x, (1, 0, 2)) for x in (q, u, v))

    odd = lax.rem(lat_index, 2)
    qv = jnp.concatenate([qt[0], vt[0]], axis=0), jnp.concatenate([qt[-1], vt[-1]], axis=0)
    toward_one = jnp.where(odd == 1, qv[1], qv[0])
    toward_two = jnp.where(odd == 1, qv[0], qv[1])
    pairs_one = shift_pairs((0, n_lat - 1), n_lon // 2)
    for a in range(1, n_lat - 1, 2):
        for z in range(n_lon):
            pairs_one += [(device(a, z), device(a + 1, z)), (device(a + 1, z), device(a, z))]
    pairs_two = [(device(a, z), device(a ^ 1, z)) for a in range(n_lat) for z in range(n_lon)]
    two = lax.ppermute(toward_two, both, pairs_two)
    one = lax.ppermute(toward_one, both, pairs_one)

    y_send = call(
        lambda *refs: inner_rows_kernel(plan, *refs),
        [(plan.y_count, width)] * n_lon,
        [(n_lon, plan.y_count, width), (planes, width), (levels, width)],
    )(qt, ut, vt)
    y_got = [y_send[0]] + [
        lax.ppermute(y_send[s], both, y_pairs(s)) for s in range(1, n_lon)
    ]

    last = jnp.concatenate([q[:, :, -1], u[:, :, -1]], axis=0)
    first = jnp.concatenate([q[:, :, 0], u[:, :, 0]], axis=0)
    west = lax.ppermute(last, "lon", [(i, (i + 1) % n_lon) for i in range(n_lon)])
    east = lax.ppermute(first, "lon", [(i, (i - 1) % n_lon) for i in range(n_lon)])

    *x_send, stepped = call(
        lambda *refs: all_rows_kernel(plan, *refs),
        [(plan.x_count, width)] * n_lon + [(rows, planes, sector)],
        [(n_lon, plan.x_count, width), (planes, width), (levels, width), (rows, planes, width)],
    )(qt, ut, vt, one, two, west, east)
    x_got = [x_send[0]] + [
        lax.ppermute(x_send[s], both, x_pairs(s)) for s in range(1, n_lon)
    ]

    hi, lo = transform_tables(plan)
    vmem = pl.BlockSpec(memory_space=pltpu.VMEM)
    smem = pl.BlockSpec(memory_space=pltpu.SMEM)

    def filtered(got, count, row_of, with_edges, pairs):
        ordered = [got[(n_lon - j) % n_lon] for j in range(n_lon)]
        pieces = call(
            lambda *refs: filter_kernel(plan, count, row_of, with_edges, *refs),
            [(count, sector)] * n_lon,
            in_specs=[smem] + [vmem] * (2 + n_lon),
        )(cutoff, hi, lo, *ordered)
        return [pieces[0]] + [
            lax.ppermute(pieces[s], both, pairs(s)) for s in range(1, n_lon)
        ]

    y_back = filtered(y_got, plan.y_count, lambda i, lat: 1 + i, True, y_pairs)
    x_back = filtered(x_got, plan.x_count, plan.x_row, False, x_pairs)
    (merged,) = call(
        lambda *refs: merge_kernel(plan, *refs),
        [(rows, planes, sector)],
        [(n_lon, max(plan.y_count, plan.x_count), sector)],
    )(stepped, *y_back, *x_back)
    return jnp.transpose(merged, (1, 0, 2)).reshape(fields, levels, rows, sector)


def solution(mesh):
    in_specs = (P(None, None, "lat", "lon"), P(None, "lat", "lon"), P(None, "lat", "lon"), P("lat"))
    out_specs = P(None, None, "lat", "lon")
    return jax.shard_map(body, mesh=mesh, in_specs=in_specs, out_specs=out_specs, check_vma=False)
```

```python
import math

import jax
import jax.numpy as jnp
from jax import lax
from jax.experimental import pallas as pl
from jax.experimental.pallas import tpu as pltpu
from jax.sharding import PartitionSpec as P

LANES = 128
EDGES = 4
FINE = 16


def padded(n):
    return -(-n // LANES) * LANES


class Plan:
    def __init__(self, fields, levels, rows, sector, n_lat, n_lon):
        self.fields, self.levels, self.rows, self.sector = fields, levels, rows, sector
        self.n_lat, self.n_lon = n_lat, n_lon
        self.planes = fields * levels
        self.circle = sector * n_lon
        self.quarter = self.circle // 4
        self.size = padded(self.quarter)
        cap = rows * n_lat // 6
        self.full = (cap - 1) // rows
        self.n_x = cap - self.full * rows
        self.n_y = rows - self.n_x
        self.width = padded(sector + EDGES)
        self.x_count = self.n_x * self.planes // n_lon
        self.y_count = self.n_y * self.planes // n_lon
        self.x_full = [0] + list(range(1 + self.n_y, rows))

    def pieces(self, index, count):
        start, out = index * self.planes, []
        stop = start + self.planes
        while start < stop:
            chunk, offset = divmod(start, count)
            size = min(count - offset, stop - start)
            out.append((chunk, offset, start - index * self.planes, size))
            start += size
        return out

    def is_full(self, lat):
        return (lat < self.full) | (lat >= self.n_lat - self.full)

    def is_part(self, lat):
        return (lat == self.full) | (lat == self.n_lat - 1 - self.full)

    def x_row(self, index, lat):
        south = lat >= self.n_lat // 2
        partial = jnp.where(south, self.rows - self.n_x + index, index)
        return jnp.where(self.is_full(lat), self.x_full[index], partial)

    def y_row(self, index, lat):
        return 1 + index


def split_speed(speed):
    return jnp.maximum(speed, 0.0), jnp.minimum(speed, 0.0)


def tiled(x, fields):
    return jnp.concatenate([x] * fields, axis=0) if fields > 1 else x


def back(x):
    return pltpu.roll(x, x.shape[1] - 1, 1)


def row_of(plan, q_ref, r):
    return q_ref[:, pl.ds(r, 1)].reshape(plan.planes, plan.sector)


def face_flux(plan, v_low, v_high, q_low, q_high):
    plus, minus = split_speed(0.5 * (v_low + v_high))
    return tiled(plus, plan.fields) * q_low + tiled(minus, plan.fields) * q_high


def first_kernel(plan, q_ref, u_ref, v_ref, *refs):
    n = plan.n_lon
    outs, (one, two, first, last, buf, q_pad, u_pad) = refs[:n], refs[n:]
    width, sector, planes = plan.width, plan.sector, plan.planes
    odd = lax.rem(lax.axis_index("lat"), 2) == 1
    lon = lax.axis_index("lon")
    lane = lax.broadcasted_iota(jnp.int32, (plan.levels, width), 1)
    inside = lane < sector - 1
    base = sector // LANES * LANES
    tail_lane = base + lax.broadcasted_iota(jnp.int32, (planes, width - base), 1)
    q_pad[...] = jnp.zeros_like(q_pad)
    u_pad[...] = jnp.zeros_like(u_pad)
    q_rows = [row_of(plan, q_ref, r) for r in range(plan.rows)]

    def south_flux(r):
        return face_flux(plan, v_ref[r], v_ref[r + 1], q_rows[r], q_rows[r + 1])

    north = south_flux(0)
    for i in range(plan.n_y):
        r = 1 + i
        q_pad[:, 0:sector] = q_rows[r]
        u_pad[:, 0:sector] = u_ref[r]
        q, u = q_pad[...], u_pad[...]
        plus, minus = split_speed(0.5 * (u + back(u)))
        plus, minus = jnp.where(inside, plus, 0.0), jnp.where(inside, minus, 0.0)
        east = tiled(plus, plan.fields) * q + tiled(minus, plan.fields) * back(q)
        stepped = q - (east - pltpu.roll(east, 1, 1))
        south = south_flux(r)
        q_pad[...] = stepped
        q_pad[:, 0:sector] = q_pad[:, 0:sector] - (south - north)
        tail = q_pad[:, base:]
        for k, value in enumerate(
            (q[:, 0:1], q[:, sector - 1 : sector], tiled(u[:, 0:1], plan.fields), tiled(u[:, sector - 1 : sector], plan.fields))
        ):
            tail = jnp.where(tail_lane == sector + k, value, tail)
        q_pad[:, base:] = tail
        for chunk, offset, start, size in plan.pieces(i, plan.y_count):
            buf[chunk, offset : offset + size, :] = q_pad[start : start + size, :]
        north = south
    for s in range(n):
        outs[s][...] = buf[lax.rem(lon + s, n)]

    one[0:planes, :] = jnp.where(odd, q_rows[-1], q_rows[0])
    one[planes:, :] = jnp.where(odd, v_ref[plan.rows - 1], v_ref[0])
    two[0:planes, :] = jnp.where(odd, q_rows[0], q_rows[-1])
    two[planes:, :] = jnp.where(odd, v_ref[0], v_ref[plan.rows - 1])
    for r in range(plan.rows):
        for out, at in ((first, 0), (last, sector - 1)):
            out[0:planes, r : r + 1] = q_rows[r][:, at : at + 1]
            out[planes:, r : r + 1] = u_ref[r][:, at : at + 1]


def ghosts(plan, one_ref, two_ref):
    lat = lax.axis_index("lat")
    odd = lax.rem(lat, 2) == 1
    sign_north = jnp.where(lat == 0, -1.0, 1.0)
    sign_south = jnp.where(lat == plan.n_lat - 1, -1.0, 1.0)
    one, two, planes = one_ref[...], two_ref[...], plan.planes
    above, below = jnp.where(odd, two, one), jnp.where(odd, one, two)
    return above[:planes], above[planes:] * sign_north, below[:planes], below[planes:] * sign_south


def lon_step(plan, q_pad, u_pad, q_row, u_row, east_column, west_column):
    sector, width, planes = plan.sector, plan.width, plan.planes
    q_pad[:, 0:sector] = q_row
    u_pad[:, 0:sector] = u_row
    q_pad[:, sector : sector + 1] = east_column[:planes]
    u_pad[:, sector : sector + 1] = east_column[planes:]
    q_pad[:, width - 1 : width] = west_column[:planes]
    u_pad[:, width - 1 : width] = west_column[planes:]
    q, u = q_pad[...], u_pad[...]
    plus, minus = split_speed(0.5 * (u + back(u)))
    east = tiled(plus, plan.fields) * q + tiled(minus, plan.fields) * back(q)
    return q - (east - pltpu.roll(east, 1, 1))


def travelling_kernel(plan, q_ref, u_ref, v_ref, one_ref, two_ref, west_ref, east_ref, *refs):
    n = plan.n_lon
    outs, (buf, q_pad, u_pad) = refs[:n], refs[n:]
    sector, rows = plan.sector, plan.rows
    lat, lon = lax.axis_index("lat"), lax.axis_index("lon")
    q_above, v_above, q_below, v_below = ghosts(plan, one_ref, two_ref)
    q_pad[...] = jnp.zeros_like(q_pad)
    u_pad[...] = jnp.zeros_like(u_pad)
    lane = lax.broadcasted_iota(jnp.int32, east_ref.shape, 1)

    def column(ref, r):
        return jnp.sum(jnp.where(lane == r, ref[...], 0.0), axis=1, keepdims=True)

    for j in range(plan.n_x):
        r = plan.x_row(j, lat)
        before, after = jnp.maximum(r - 1, 0), jnp.minimum(r + 1, rows - 1)
        top, bottom = r == 0, r == rows - 1
        q_row, v_row = row_of(plan, q_ref, r), v_ref[r]
        stepped = lon_step(plan, q_pad, u_pad, q_row, u_ref[r], column(east_ref, r), column(west_ref, r))
        south = face_flux(
            plan,
            v_row,
            jnp.where(bottom, v_below, v_ref[after]),
            q_row,
            jnp.where(bottom, q_below, row_of(plan, q_ref, after)),
        )
        north = face_flux(
            plan,
            jnp.where(top, v_above, v_ref[before]),
            v_row,
            jnp.where(top, q_above, row_of(plan, q_ref, before)),
            q_row,
        )
        q_pad[...] = stepped
        q_pad[:, 0:sector] = q_pad[:, 0:sector] - (south - north)
        for chunk, offset, start, size in plan.pieces(j, plan.x_count):
            buf[chunk, offset : offset + size, :] = q_pad[start : start + size, :]
    for s in range(n):
        outs[s][...] = buf[lax.rem(lon + s, n)]


def rest_kernel(plan, q_ref, u_ref, v_ref, one_ref, two_ref, west_ref, east_ref, out, q_pad, u_pad):
    sector, rows = plan.sector, plan.rows

    @pl.when(jnp.logical_not(plan.is_full(lax.axis_index("lat"))))
    def _():
        q_above, v_above, q_below, v_below = ghosts(plan, one_ref, two_ref)
        q_pad[...] = jnp.zeros_like(q_pad)
        u_pad[...] = jnp.zeros_like(u_pad)
        north = face_flux(plan, v_above, v_ref[0], q_above, row_of(plan, q_ref, 0))
        for r in range(rows):
            q_row = row_of(plan, q_ref, r)
            stepped = lon_step(
                plan, q_pad, u_pad, q_row, u_ref[r], east_ref[:, r : r + 1], west_ref[:, r : r + 1]
            )
            inner = r + 1 < rows
            south = face_flux(
                plan,
                v_ref[r],
                v_ref[r + 1] if inner else v_below,
                q_row,
                row_of(plan, q_ref, r + 1) if inner else q_below,
            )
            value = stepped[:, 0:sector] - (south - north)
            out[:, r : r + 1] = value.reshape(plan.fields, 1, plan.levels, sector)
            north = south


def turn(numerator, circle):
    p = numerator - circle * jnp.floor(numerator * (1.0 / circle))
    j = jnp.floor(p * (4.0 / circle) + 0.5)
    x = (p - j * (circle / 4)) * (2.0 * math.pi / circle)
    z = x * x
    s = x * (1 + z * (-1 / 6 + z * (1 / 120 + z * (-1 / 5040 + z * (1 / 362880)))))
    c = 1 + z * (-1 / 2 + z * (1 / 24 + z * (-1 / 720 + z * (1 / 40320 + z * (-1 / 3628800)))))
    swap = (j == 1.0) | (j == 3.0)
    cos, sin = jnp.where(swap, s, c), jnp.where(swap, c, s)
    cos = jnp.where((j == 1.0) | (j == 2.0), -cos, cos)
    sin = jnp.where((j == 2.0) | (j == 3.0), -sin, sin)
    return cos, sin


def table_kernel(plan, even_hi, even_lo, odd_hi, odd_lo):
    size = plan.size
    coarse = size // FINE

    def numerators(count, step, r):
        n = step * lax.broadcasted_iota(jnp.int32, (count, size), 0)
        k = 4 * lax.broadcasted_iota(jnp.int32, (count, size), 1) + r
        return (n * k).astype(jnp.float32)

    def put(hi, lo, index, value):
        high = value.astype(jnp.bfloat16)
        hi[index] = high
        lo[index] = (value - high.astype(jnp.float32)).astype(jnp.bfloat16)

    for r in range(4):
        cos_c, sin_c = turn(numerators(coarse, FINE, r), plan.circle)
        cos_f, sin_f = turn(numerators(FINE, 1, r), plan.circle)
        sum_f, gap_f = cos_f + sin_f, cos_f - sin_f
        column = slice(0, size) if r < 2 else slice(size, 2 * size)
        for i in range(coarse):
            c, s = cos_c[i : i + 1], sin_c[i : i + 1]
            rows = slice(i * FINE, (i + 1) * FINE)
            plus = c * sum_f + s * gap_f
            if r % 2 == 0:
                put(even_hi, even_lo, (r // 2, rows), plus)
            else:
                minus = c * gap_f - s * sum_f
                put(odd_hi, odd_lo, (rows, column), plus)
                rows = slice(size + i * FINE, size + (i + 1) * FINE)
                put(odd_hi, odd_lo, (rows, column), minus if r == 1 else -minus)


def product(x, table_hi, table_lo, transposed):
    dims = (((1,), (1 if transposed else 0,)), ((), ()))
    x_hi = x.astype(jnp.bfloat16)
    x_lo = (x - x_hi.astype(jnp.float32)).astype(jnp.bfloat16)
    count = x.shape[0]
    both = lax.dot_general(
        jnp.concatenate([x_hi, x_lo], axis=0), table_hi, dims, preferred_element_type=jnp.float32
    )
    low = lax.dot_general(x_hi, table_lo, dims, preferred_element_type=jnp.float32)
    return both[:count] + both[count:] + low


def filter_quarters(plan, quarters, cut, even_hi, even_lo, odd_hi, odd_lo):
    x0, x1, x2, x3 = quarters
    size, circle = plan.size, plan.circle
    a, b, odd = x0 + x2, x1 + x3, jnp.concatenate([x0 - x2, x1 - x3], axis=1)

    def kept(h, k, m):
        ok = (jnp.minimum(k, circle - k) <= cut) & (m < plan.quarter)
        return jnp.where(ok, h, 0.0) * (1.0 / circle)

    m = lax.broadcasted_iota(jnp.int32, x0.shape, 1)
    lane = lax.broadcasted_iota(jnp.int32, odd.shape, 1)
    m_odd = jnp.where(lane < size, lane, lane - size)
    k_odd = 4 * m_odd + jnp.where(lane < size, 1, 3)
    tables = [(even_hi[0], even_lo[0]), (even_hi[1], even_lo[1]), (odd_hi[...], odd_lo[...])]
    h0 = kept(product(a + b, *tables[0], False), 4 * m, m)
    h2 = kept(product(a - b, *tables[1], False), 4 * m + 2, m)
    h13 = kept(product(odd, *tables[2], False), k_odd, m_odd)
    even, twice = product(h0, *tables[0], True), product(h2, *tables[1], True)
    other = product(h13, *tables[2], True)
    both, apart = even + twice, even - twice
    o_u, o_v = other[:, :size], other[:, size:]
    return both + o_u, apart + o_v, both - o_u, apart - o_v


def filter_kernel(plan, count, rows_here, row_index, with_edges, needed, cut_ref, *refs):
    n = plan.n_lon
    tables, ins, outs = refs[:4], refs[4 : 4 + n], refs[4 + n :]
    sector, width = plan.sector, plan.width
    lat, lon = lax.axis_index("lat"), lax.axis_index("lon")

    @pl.when(needed(lat))
    def _():
        circle_index = lon * count + lax.broadcasted_iota(jnp.int32, (count, 1), 0)
        cut = jnp.full((count, 1), plan.circle, jnp.int32)
        for i in range(rows_here):
            here = (circle_index >= i * plan.planes) & (circle_index < (i + 1) * plan.planes)
            cut = jnp.where(here, cut_ref[row_index(i, lat)], cut)
        lane = lax.broadcasted_iota(jnp.int32, (count, width), 1)
        pieces = [jnp.where(lane < sector, ref[...], 0.0) for ref in ins]
        if with_edges:
            tails = [ref[:, sector : sector + EDGES] for ref in ins]
            fluxes = []
            for j in range(n):
                here, there = tails[j], tails[(j + 1) % n]
                plus, minus = split_speed(0.5 * (here[:, 3:4] + there[:, 2:3]))
                fluxes.append(plus * here[:, 1:2] + minus * there[:, 0:1])
            pieces = [
                piece
                - jnp.where(lane == sector - 1, fluxes[j], 0.0)
                + jnp.where(lane == 0, fluxes[j - 1], 0.0)
                for j, piece in enumerate(pieces)
            ]
        per = n // 4
        if per == 1 and width == plan.size:
            quarters = pieces
        else:
            spare = [jnp.zeros((count, plan.size - plan.quarter), jnp.float32)] * (plan.size > plan.quarter)
            quarters = [
                jnp.concatenate([p[:, :sector] for p in pieces[per * i : per * (i + 1)]] + spare, axis=1)
                for i in range(4)
            ]
        filtered = filter_quarters(plan, quarters, cut, *tables)
        for j in range(n):
            part = j % per
            outs[j][:, 0:sector] = filtered[j // per][:, part * sector : (part + 1) * sector]


def place_kernel(plan, count, rows_here, row_index, needed, whole, *refs):
    n = plan.n_lon
    ins, (out, buf, row_buf, sems) = refs[:n], refs[n:]
    lat, lon = lax.axis_index("lat"), lax.axis_index("lon")

    @pl.when(needed(lat))
    def _():
        for j in range(n):
            buf[lax.rem(lon + n - j, n)] = ins[j][...]
        copies = []
        for i in range(rows_here):
            for chunk, offset, start, size in plan.pieces(i, count):
                row_buf[i, start : start + size, :] = buf[chunk, offset : offset + size, 0 : plan.sector]
            for f in range(plan.fields):
                copies.append(
                    pltpu.make_async_copy(
                        row_buf.at[i, pl.ds(f * plan.levels, plan.levels)],
                        out.at[f, row_index(i, lat)],
                        sems.at[i, f],
                    )
                )
                copies[-1].start()
        for copy in copies:
            copy.wait()


def f32(*shape):
    return jax.ShapeDtypeStruct(shape, jnp.float32)


def vmem(*shape):
    return pltpu.VMEM(shape, jnp.float32)


def body(tracers, zonal_wind, meridional_wind, cutoff):
    fields, levels, rows, sector = tracers.shape
    n_lat, n_lon = lax.axis_size("lat"), lax.axis_size("lon")
    plan = Plan(fields, levels, rows, sector, n_lat, n_lon)
    planes, width, size = plan.planes, plan.width, plan.size
    q = jnp.transpose(tracers, (0, 2, 1, 3))
    u, v = (jnp.transpose(x, (1, 0, 2)) for x in (zonal_wind, meridional_wind))
    both = ("lat", "lon")

    def device(lat, lon):
        return lat * n_lon + lon % n_lon

    def shift_pairs(lats, by):
        return [(device(a, z), device(a, z + by)) for a in lats for z in range(n_lon)]

    def x_pairs(by):
        return shift_pairs(range(n_lat), by)

    def swapped(a, b):
        return [(device(p, z), device(q, z)) for p, q in ((a, b), (b, a)) for z in range(n_lon)]

    def y_pairs(by):
        spare = list(range(plan.full + 1, n_lat - plan.full - 1))
        pairs = shift_pairs(list(range(plan.full)) + list(range(n_lat - plan.full, n_lat)), by)
        pairs += swapped(plan.full, n_lat - 1 - plan.full)
        for a, b in zip(spare[0::2], spare[1::2]):
            pairs += swapped(a, b)
        return pairs

    pairs_one = shift_pairs((0, n_lat - 1), n_lon // 2)
    for a in range(1, n_lat - 1, 2):
        pairs_one += swapped(a, a + 1)
    pairs_two = [pair for a in range(0, n_lat, 2) for pair in swapped(a, a + 1)]

    *y_send, to_one, to_two, first, last = pl.pallas_call(
        lambda *refs: first_kernel(plan, *refs),
        out_shape=[f32(plan.y_count, width)] * n_lon
        + [f32(planes + levels, sector)] * 2
        + [f32(planes + levels, rows)] * 2,
        scratch_shapes=[vmem(n_lon, plan.y_count, width), vmem(planes, width), vmem(levels, width)],
        name="inner",
    )(q, u, v)
    y_got = [y_send[0]] + [lax.ppermute(y_send[s], both, y_pairs(s)) for s in range(1, n_lon)]
    two = lax.ppermute(to_two, both, pairs_two)
    one = lax.ppermute(to_one, both, pairs_one)
    west = lax.ppermute(last, both, x_pairs(1))
    east = lax.ppermute(first, both, x_pairs(-1))

    *x_send, = pl.pallas_call(
        lambda *refs: travelling_kernel(plan, *refs),
        out_shape=[f32(plan.x_count, width)] * n_lon,
        scratch_shapes=[vmem(n_lon, plan.x_count, width), vmem(planes, width), vmem(levels, width)],
        name="travel",
    )(q, u, v, one, two, west, east)
    x_got = [x_send[0]] + [lax.ppermute(x_send[s], both, x_pairs(s)) for s in range(1, n_lon)]

    out = pl.pallas_call(
        lambda *refs: rest_kernel(plan, *refs),
        out_shape=f32(fields, rows, levels, sector),
        scratch_shapes=[vmem(planes, width), vmem(levels, width)],
        name="rest",
    )(q, u, v, one, two, west, east)

    tables = pl.pallas_call(
        lambda *refs: table_kernel(plan, *refs),
        out_shape=[jax.ShapeDtypeStruct((2, size, size), jnp.bfloat16)] * 2
        + [jax.ShapeDtypeStruct((2 * size, 2 * size), jnp.bfloat16)] * 2,
        name="tables",
    )()
    whole = pl.BlockSpec(memory_space=pltpu.VMEM)
    smem = pl.BlockSpec(memory_space=pltpu.SMEM)
    anywhere = pl.BlockSpec(memory_space=pl.ANY)

    def filtered(got, count, rows_here, row_index, with_edges, needed, pairs, name):
        ordered = [got[(n_lon - j) % n_lon] for j in range(n_lon)]
        pieces = pl.pallas_call(
            lambda *refs: filter_kernel(plan, count, rows_here, row_index, with_edges, needed, *refs),
            out_shape=[f32(count, width)] * n_lon,
            in_specs=[smem] + [whole] * (4 + n_lon),
            name=name,
        )(cutoff, *tables, *ordered)
        return [pieces[0]] + [lax.ppermute(pieces[s], both, pairs(s)) for s in range(1, n_lon)]

    def placed(out, pieces, count, rows_here, row_index, needed, name):
        return pl.pallas_call(
            lambda *refs: place_kernel(plan, count, rows_here, row_index, needed, *refs),
            out_shape=f32(fields, rows, levels, sector),
            in_specs=[anywhere] + [whole] * n_lon,
            out_specs=anywhere,
            scratch_shapes=[
                vmem(n_lon, count, width),
                vmem(rows_here, planes, sector),
                pltpu.SemaphoreType.DMA((rows_here, fields)),
            ],
            input_output_aliases={0: 0},
            name=name,
        )(out, *pieces)

    def polar(lat):
        return plan.is_full(lat) | plan.is_part(lat)

    y_args = plan.y_count, plan.n_y, plan.y_row
    x_args = plan.x_count, plan.n_x, plan.x_row
    y_back = filtered(y_got, *y_args, True, plan.is_full, y_pairs, "filter_y")
    x_back = filtered(x_got, *x_args, False, polar, x_pairs, "filter_x")
    out = placed(out, y_back, *y_args, plan.is_full, "place_y")
    out = placed(out, x_back, *x_args, polar, "place_x")
    return jnp.transpose(out, (0, 2, 1, 3))


def solution(mesh):
    in_specs = (P(None, None, "lat", "lon"), P(None, "lat", "lon"), P(None, "lat", "lon"), P("lat"))
    out_specs = P(None, None, "lat", "lon")
    return jax.shard_map(body, mesh=mesh, in_specs=in_specs, out_specs=out_specs, check_vma=False)
```

```python
import math

import jax
import jax.numpy as jnp
from jax import lax
from jax.experimental import pallas as pl
from jax.experimental.pallas import tpu as pltpu
from jax.sharding import PartitionSpec as P

LANES = 128
EDGES = 4
FINE = 16
SUMS = 3


def padded(n):
    return -(-n // LANES) * LANES


class Plan:
    def __init__(self, fields, levels, rows, sector, n_lat, n_lon):
        self.fields, self.levels, self.rows, self.sector = fields, levels, rows, sector
        self.n_lat, self.n_lon = n_lat, n_lon
        self.planes = fields * levels
        self.circle = sector * n_lon
        self.quarter = self.circle // 4
        self.size = padded(self.quarter)
        cap = rows * n_lat // 6
        self.full = (cap - 1) // rows
        self.n_x = cap - self.full * rows
        self.apart = self.full == 1
        self.n_y = rows - self.n_x - self.apart
        self.width = padded(sector + EDGES)
        self.x_count = self.share(self.n_x)
        self.y_count = self.share(self.n_y)
        self.x_full = list(range(1 + self.n_y, rows))
        if not self.apart:
            self.x_full = [0] + self.x_full
        self.edge = padded(self.planes + levels)
        self.sum_groups = -(-self.planes // self.x_count)

    def share(self, rows):
        return -(-rows * self.planes // (8 * self.n_lon)) * 8

    def pieces(self, index, count):
        start, out = index * self.planes, []
        stop = start + self.planes
        while start < stop:
            chunk, offset = divmod(start, count)
            size = min(count - offset, stop - start)
            out.append((chunk, offset, start - index * self.planes, size))
            start += size
        return out

    def is_full(self, lat):
        return (lat < self.full) | (lat >= self.n_lat - self.full)

    def is_part(self, lat):
        return (lat == self.full) | (lat == self.n_lat - 1 - self.full)

    def x_row(self, index, lat):
        south = lat >= self.n_lat // 2
        partial = jnp.where(south, self.rows - self.n_x + index, index)
        full = jnp.where(south & self.apart, index, self.x_full[index])
        return jnp.where(self.is_full(lat), full, partial)

    def y_row(self, index, lat):
        south = lat >= self.n_lat // 2
        return jnp.where(south & self.apart, self.n_x + index, 1 + index)

    def pole_row(self, lat):
        return jnp.where(lat >= self.n_lat // 2, self.rows - 1, 0)


def split_speed(speed):
    return jnp.maximum(speed, 0.0), jnp.minimum(speed, 0.0)


def tiled(x, fields):
    return jnp.concatenate([x] * fields, axis=0) if fields > 1 else x


def back(x):
    return pltpu.roll(x, x.shape[1] - 1, 1)


def row_of(plan, q_ref, r):
    return q_ref[:, pl.ds(r, 1)].reshape(plan.planes, plan.sector)


def face_flux(plan, v_low, v_high, q_low, q_high):
    plus, minus = split_speed(0.5 * (v_low + v_high))
    return tiled(plus, plan.fields) * q_low + tiled(minus, plan.fields) * q_high


def emit(plan, buf, q_pad, u_pad, index, count, q_row, u_row, lat_divergence):
    sector, width, fields = plan.sector, plan.width, plan.fields
    q_pad[:, 0:sector] = q_row
    u_pad[:, 0:sector] = u_row
    q, u = q_pad[...], u_pad[...]
    inside = lax.broadcasted_iota(jnp.int32, u.shape, 1) < sector - 1
    plus, minus = split_speed(0.5 * (u + back(u)))
    plus, minus = jnp.where(inside, plus, 0.0), jnp.where(inside, minus, 0.0)
    east = tiled(plus, fields) * q + tiled(minus, fields) * back(q)
    q_pad[...] = q - (east - pltpu.roll(east, 1, 1))
    q_pad[:, 0:sector] = q_pad[:, 0:sector] - lat_divergence
    base = sector // LANES * LANES
    tail = q_pad[:, base:]
    lane = base + lax.broadcasted_iota(jnp.int32, tail.shape, 1)
    edges = q[:, 0:1], q[:, sector - 1 : sector], u[:, 0:1], u[:, sector - 1 : sector]
    for k, value in enumerate(edges):
        tail = jnp.where(lane == sector + k, value if k < 2 else tiled(value, fields), tail)
    q_pad[:, base:] = tail
    for chunk, offset, start, size in plan.pieces(index, count):
        buf[chunk, offset : offset + size, :] = q_pad[start : start + size, :]


def hand_out(plan, buf, outs):
    lon = lax.axis_index("lon")
    for s in range(plan.n_lon):
        outs[s][...] = buf[lax.rem(lon + s, plan.n_lon)]


def inner_kernel(plan, q_ref, u_ref, v_ref, *refs):
    outs, (two, buf, q_pad, u_pad) = refs[: plan.n_lon], refs[plan.n_lon :]
    planes, rows = plan.planes, plan.rows
    lat = lax.axis_index("lat")
    q_pad[...] = jnp.zeros_like(q_pad)
    u_pad[...] = jnp.zeros_like(u_pad)
    first = plan.y_row(0, lat)

    def south_flux(r):
        return face_flux(plan, v_ref[r], v_ref[r + 1], row_of(plan, q_ref, r), row_of(plan, q_ref, r + 1))

    north = south_flux(first - 1)
    for i in range(plan.n_y):
        r = first + i
        south = south_flux(r)
        emit(plan, buf, q_pad, u_pad, i, plan.y_count, row_of(plan, q_ref, r), u_ref[r], south - north)
        north = south
    hand_out(plan, buf, outs)
    r = jnp.where(lax.rem(lat, 2) == 1, 0, rows - 1)
    two[0:planes, :] = row_of(plan, q_ref, r)
    two[planes:, :] = v_ref[r]


def ghosts(plan, one_ref, two_ref):
    lat = lax.axis_index("lat")
    odd = lax.rem(lat, 2) == 1
    sign_north = jnp.where(lat == 0, -1.0, 1.0)
    sign_south = jnp.where(lat == plan.n_lat - 1, -1.0, 1.0)
    one, two, planes = one_ref[...], two_ref[...], plan.planes
    above, below = jnp.where(odd, two, one), jnp.where(odd, one, two)
    return above[:planes], above[planes:] * sign_north, below[:planes], below[planes:] * sign_south


def lat_divergence(plan, q_ref, v_ref, r, around):
    q_above, v_above, q_below, v_below = around
    rows = plan.rows
    before, after = jnp.maximum(r - 1, 0), jnp.minimum(r + 1, rows - 1)
    top, bottom = r == 0, r == rows - 1
    q_row, v_row = row_of(plan, q_ref, r), v_ref[r]
    v_south = jnp.where(bottom, v_below, v_ref[after])
    q_south = jnp.where(bottom, q_below, row_of(plan, q_ref, after))
    v_north = jnp.where(top, v_above, v_ref[before])
    q_north = jnp.where(top, q_above, row_of(plan, q_ref, before))
    south = face_flux(plan, v_row, v_south, q_row, q_south)
    return south - face_flux(plan, v_north, v_row, q_north, q_row)


def travelling_kernel(plan, q_ref, u_ref, v_ref, two_ref, one_ref, *refs):
    n = plan.n_lon
    outs, (to_one, first, last, buf, q_pad, u_pad, columns) = refs[:n], refs[n:]
    planes, sector, rows = plan.planes, plan.sector, plan.rows
    lat = lax.axis_index("lat")
    around = ghosts(plan, one_ref, two_ref)
    q_pad[...] = jnp.zeros_like(q_pad)
    u_pad[...] = jnp.zeros_like(u_pad)
    for j in range(plan.n_x):
        r = plan.x_row(j, lat)
        divergence = lat_divergence(plan, q_ref, v_ref, r, around)
        emit(plan, buf, q_pad, u_pad, j, plan.x_count, row_of(plan, q_ref, r), u_ref[r], divergence)
    hand_out(plan, buf, outs)
    r = jnp.where(lax.rem(lat, 2) == 1, rows - 1, 0)
    if to_one is not None:
        to_one[0:planes, :] = row_of(plan, q_ref, r)
        to_one[planes:, :] = v_ref[r]
    columns[...] = jnp.zeros_like(columns)
    for out, at in ((first, 0), (last, sector - 1)):
        for r in range(rows):
            columns[0:planes, r : r + 1] = row_of(plan, q_ref, r)[:, at : at + 1]
            columns[planes : planes + plan.levels, r : r + 1] = u_ref[r][:, at : at + 1]
        out[...] = columns[...].T[: out.shape[0]]


def lon_step(plan, q_pad, u_pad, q_row, u_row, east_column, west_column):
    sector, width, planes = plan.sector, plan.width, plan.planes
    q_pad[:, 0:sector] = q_row
    u_pad[:, 0:sector] = u_row
    q_pad[:, sector : sector + 1] = east_column[:planes]
    u_pad[:, sector : sector + 1] = east_column[planes : planes + plan.levels]
    q_pad[:, width - 1 : width] = west_column[:planes]
    u_pad[:, width - 1 : width] = west_column[planes : planes + plan.levels]
    q, u = q_pad[...], u_pad[...]
    plus, minus = split_speed(0.5 * (u + back(u)))
    east = tiled(plus, plan.fields) * q + tiled(minus, plan.fields) * back(q)
    return q - (east - pltpu.roll(east, 1, 1))


def sector_turns(plan, shape):
    at = lax.axis_index("lon") * plan.sector + lax.broadcasted_iota(jnp.int32, shape, 1)
    return turn(at.astype(jnp.float32), plan.circle)


def rest_kernel(plan, q_ref, u_ref, v_ref, one_ref, two_ref, west_ref, east_ref, out, sums, q_pad, u_pad, stage, pack, sem):
    sector, rows, planes = plan.sector, plan.rows, plan.planes
    lat = lax.axis_index("lat")
    around = q_above, v_above, q_below, v_below = ghosts(plan, one_ref, two_ref)
    q_pad[...] = jnp.zeros_like(q_pad)
    u_pad[...] = jnp.zeros_like(u_pad)
    pack[...] = jnp.zeros_like(pack)
    pack[0 : east_ref.shape[0], :] = east_ref[...]
    east_columns = pack[...].T
    pack[0 : west_ref.shape[0], :] = west_ref[...]
    west_columns = pack[...].T

    @pl.when(jnp.logical_not(plan.is_full(lat)))
    def _():
        north = face_flux(plan, v_above, v_ref[0], q_above, row_of(plan, q_ref, 0))
        for r in range(rows):
            q_row = row_of(plan, q_ref, r)
            stepped = lon_step(
                plan, q_pad, u_pad, q_row, u_ref[r], east_columns[:, r : r + 1], west_columns[:, r : r + 1]
            )
            inner = r + 1 < rows
            south = face_flux(
                plan,
                v_ref[r],
                v_ref[r + 1] if inner else v_below,
                q_row,
                row_of(plan, q_ref, r + 1) if inner else q_below,
            )
            value = stepped[:, 0:sector] - (south - north)
            stage[:, r : r + 1] = value.reshape(plan.fields, 1, plan.levels, sector)
            north = south
        copy = pltpu.make_async_copy(stage, out, sem)
        copy.start()
        copy.wait()

    if plan.apart:

        @pl.when(plan.is_full(lat))
        def _():
            r = plan.pole_row(lat)
            lane = lax.broadcasted_iota(jnp.int32, east_columns.shape, 1)

            def column(columns):
                return jnp.sum(jnp.where(lane == r, columns, 0.0), axis=1, keepdims=True)

            stepped = lon_step(
                plan, q_pad, u_pad, row_of(plan, q_ref, r), u_ref[r], column(east_columns), column(west_columns)
            )
            value = stepped[:, 0:sector] - lat_divergence(plan, q_ref, v_ref, r, around)
            cos, sin = sector_turns(plan, (1, sector))
            for k, part in enumerate((value, value * cos, value * sin)):
                sums[:, k : k + 1] = jnp.sum(part, axis=1, keepdims=True)


def turn(numerator, circle):
    p = numerator - circle * jnp.floor(numerator * (1.0 / circle))
    j = jnp.floor(p * (4.0 / circle) + 0.5)
    x = (p - j * (circle / 4)) * (2.0 * math.pi / circle)
    z = x * x
    s = x * (1 + z * (-1 / 6 + z * (1 / 120 + z * (-1 / 5040 + z * (1 / 362880)))))
    c = 1 + z * (-1 / 2 + z * (1 / 24 + z * (-1 / 720 + z * (1 / 40320 + z * (-1 / 3628800)))))
    swap = (j == 1.0) | (j == 3.0)
    cos, sin = jnp.where(swap, s, c), jnp.where(swap, c, s)
    cos = jnp.where((j == 1.0) | (j == 2.0), -cos, cos)
    sin = jnp.where((j == 2.0) | (j == 3.0), -sin, sin)
    return cos, sin


def table_kernel(plan, even_hi, even_lo, odd_hi, odd_lo):
    size = plan.size
    coarse = size // FINE

    def numerators(count, step, r):
        n = step * lax.broadcasted_iota(jnp.int32, (count, size), 0)
        k = 4 * lax.broadcasted_iota(jnp.int32, (count, size), 1) + r
        return (n * k).astype(jnp.float32)

    def put(hi, lo, index, value):
        high = value.astype(jnp.bfloat16)
        hi[index] = high
        lo[index] = (value - high.astype(jnp.float32)).astype(jnp.bfloat16)

    for r in range(4):
        cos_c, sin_c = turn(numerators(coarse, FINE, r), plan.circle)
        cos_f, sin_f = turn(numerators(FINE, 1, r), plan.circle)
        sum_f, gap_f = cos_f + sin_f, cos_f - sin_f
        column = slice(0, size) if r < 2 else slice(size, 2 * size)
        for i in range(coarse):
            c, s = cos_c[i : i + 1], sin_c[i : i + 1]
            rows = slice(i * FINE, (i + 1) * FINE)
            plus = c * sum_f + s * gap_f
            if r % 2 == 0:
                put(even_hi, even_lo, (r // 2, rows), plus)
            else:
                minus = c * gap_f - s * sum_f
                put(odd_hi, odd_lo, (rows, column), plus)
                rows = slice(size + i * FINE, size + (i + 1) * FINE)
                put(odd_hi, odd_lo, (rows, column), minus if r == 1 else -minus)


def product(x, table_hi, table_lo, transposed):
    dims = (((1,), (1 if transposed else 0,)), ((), ()))
    x_hi = x.astype(jnp.bfloat16)
    x_lo = (x - x_hi.astype(jnp.float32)).astype(jnp.bfloat16)
    count = x.shape[0]
    both = lax.dot_general(
        jnp.concatenate([x_hi, x_lo], axis=0), table_hi, dims, preferred_element_type=jnp.float32
    )
    low = lax.dot_general(x_hi, table_lo, dims, preferred_element_type=jnp.float32)
    return both[:count] + both[count:] + low


def filter_quarters(plan, quarters, cut, even_hi, even_lo, odd_hi, odd_lo):
    x0, x1, x2, x3 = quarters
    size, circle = plan.size, plan.circle
    a, b, odd = x0 + x2, x1 + x3, jnp.concatenate([x0 - x2, x1 - x3], axis=1)

    def kept(h, k, m):
        ok = (jnp.minimum(k, circle - k) <= cut) & (m < plan.quarter)
        return jnp.where(ok, h, 0.0) * (1.0 / circle)

    m = lax.broadcasted_iota(jnp.int32, x0.shape, 1)
    lane = lax.broadcasted_iota(jnp.int32, odd.shape, 1)
    m_odd = jnp.where(lane < size, lane, lane - size)
    k_odd = 4 * m_odd + jnp.where(lane < size, 1, 3)
    tables = [(even_hi[0], even_lo[0]), (even_hi[1], even_lo[1]), (odd_hi[...], odd_lo[...])]
    h0 = kept(product(a + b, *tables[0], False), 4 * m, m)
    h2 = kept(product(a - b, *tables[1], False), 4 * m + 2, m)
    h13 = kept(product(odd, *tables[2], False), k_odd, m_odd)
    even, twice = product(h0, *tables[0], True), product(h2, *tables[1], True)
    other = product(h13, *tables[2], True)
    both, apart = even + twice, even - twice
    o_u, o_v = other[:, :size], other[:, size:]
    return both + o_u, apart + o_v, both - o_u, apart - o_v


def filter_kernel(plan, count, rows_here, row_index, needed, with_sums, cut_ref, *refs):
    n = plan.n_lon
    tables, ins, outs = refs[:4], refs[4 : 4 + n], refs[-n:]
    sector, width = plan.sector, plan.width
    lat, lon = lax.axis_index("lat"), lax.axis_index("lon")

    @pl.when(needed(lat))
    def _():
        circle_index = lon * count + lax.broadcasted_iota(jnp.int32, (count, 1), 0)
        cut = jnp.full((count, 1), plan.circle, jnp.int32)
        for i in range(rows_here):
            here = (circle_index >= i * plan.planes) & (circle_index < (i + 1) * plan.planes)
            cut = jnp.where(here, cut_ref[row_index(i, lat)], cut)
        lane = lax.broadcasted_iota(jnp.int32, (count, width), 1)
        pieces = [jnp.where(lane < sector, ref[...], 0.0) for ref in ins]
        tails = [ref[:, sector : sector + EDGES] for ref in ins]
        fluxes = []
        for j in range(n):
            here, there = tails[j], tails[(j + 1) % n]
            plus, minus = split_speed(0.5 * (here[:, 3:4] + there[:, 2:3]))
            fluxes.append(plus * here[:, 1:2] + minus * there[:, 0:1])
        pieces = [
            piece
            - jnp.where(lane == sector - 1, fluxes[j], 0.0)
            + jnp.where(lane == 0, fluxes[j - 1], 0.0)
            for j, piece in enumerate(pieces)
        ]
        per = n // 4
        if per == 1 and width == plan.size:
            quarters = pieces
        else:
            spare = [jnp.zeros((count, plan.size - plan.quarter), jnp.float32)] * (plan.size > plan.quarter)
            quarters = [
                jnp.concatenate([p[:, :sector] for p in pieces[per * i : per * (i + 1)]] + spare, axis=1)
                for i in range(4)
            ]
        filtered = filter_quarters(plan, quarters, cut, *tables)
        for j in range(n):
            part = j % per
            outs[j][:, 0:sector] = filtered[j // per][:, part * sector : (part + 1) * sector]
        if with_sums:
            sums = refs[4 + n]
            for g in range(plan.sum_groups):
                size = min(count, plan.planes - g * count)
                at = sector + SUMS * g
                for j in range(n):
                    outs[j][0:size, at : at + SUMS] = sums[g * count : g * count + size, 0:SUMS]


def place_kernel(plan, count, rows_here, row_index, needed, with_sums, whole, *refs):
    n = plan.n_lon
    ins, (out, buf, row_buf, sems) = refs[:n], refs[n:]
    lat, lon = lax.axis_index("lat"), lax.axis_index("lon")

    def send(i, row):
        copies = [
            pltpu.make_async_copy(
                row_buf.at[i, pl.ds(f * plan.levels, plan.levels)], out.at[f, row], sems.at[i, f]
            )
            for f in range(plan.fields)
        ]
        for copy in copies:
            copy.start()
        return copies

    if with_sums:

        @pl.when(plan.is_full(lat))
        def _():
            i = rows_here
            cos, sin = sector_turns(plan, (1, plan.sector))
            for g in range(plan.sum_groups):
                size = min(count, plan.planes - g * count)
                at = plan.sector + SUMS * g
                total = sum(ref[0:size, at : at + SUMS] for ref in ins)
                row_buf[i, g * count : g * count + size, :] = (
                    total[:, 0:1] + 2.0 * (total[:, 1:2] * cos + total[:, 2:3] * sin)
                ) * (1.0 / plan.circle)
            for copy in send(i, plan.pole_row(lat)):
                copy.wait()

    @pl.when(needed(lat))
    def _():
        for j in range(n):
            buf[lax.rem(lon + n - j, n)] = ins[j][...]
        copies = []
        for i in range(rows_here):
            for chunk, offset, start, size in plan.pieces(i, count):
                row_buf[i, start : start + size, :] = buf[chunk, offset : offset + size, 0 : plan.sector]
            copies += send(i, row_index(i, lat))
        for copy in copies:
            copy.wait()


def f32(*shape):
    return jax.ShapeDtypeStruct(shape, jnp.float32)


def vmem(*shape):
    return pltpu.VMEM(shape, jnp.float32)


def body(tracers, zonal_wind, meridional_wind, cutoff):
    fields, levels, rows, sector = tracers.shape
    n_lat, n_lon = lax.axis_size("lat"), lax.axis_size("lon")
    plan = Plan(fields, levels, rows, sector, n_lat, n_lon)
    planes, width, size = plan.planes, plan.width, plan.size
    q = jnp.transpose(tracers, (0, 2, 1, 3))
    u, v = (jnp.transpose(x, (1, 0, 2)) for x in (zonal_wind, meridional_wind))
    both = ("lat", "lon")

    def device(lat, lon):
        return lat * n_lon + lon % n_lon

    def shift_pairs(lats, by):
        return [(device(a, z), device(a, z + by)) for a in lats for z in range(n_lon)]

    def x_pairs(by):
        return shift_pairs(range(n_lat), by)

    def swapped(a, b):
        return [(device(p, z), device(q, z)) for p, q in ((a, b), (b, a)) for z in range(n_lon)]

    def y_pairs(by):
        spare = list(range(plan.full + 1, n_lat - plan.full - 1))
        pairs = shift_pairs(list(range(plan.full)) + list(range(n_lat - plan.full, n_lat)), by)
        pairs += swapped(plan.full, n_lat - 1 - plan.full)
        for a, b in zip(spare[0::2], spare[1::2]):
            pairs += swapped(a, b)
        return pairs

    pairs_one = shift_pairs((0, n_lat - 1), n_lon // 2)
    for a in range(1, n_lat - 1, 2):
        pairs_one += swapped(a, a + 1)
    pairs_two = [pair for a in range(0, n_lat, 2) for pair in swapped(a, a + 1)]

    whole = pl.BlockSpec(memory_space=pltpu.VMEM)
    smem = pl.BlockSpec(memory_space=pltpu.SMEM)
    anywhere = pl.BlockSpec(memory_space=pl.ANY)
    row_pads = [vmem(planes, width), vmem(levels, width)]
    row_pair = f32(planes + levels, sector)

    *y_send, to_two = pl.pallas_call(
        lambda *refs: inner_kernel(plan, *refs),
        out_shape=[f32(plan.y_count, width)] * n_lon + [row_pair],
        scratch_shapes=[vmem(n_lon, plan.y_count, width), *row_pads],
        name="inner",
    )(q, u, v)
    two = lax.ppermute(to_two, both, pairs_two)
    y_got = [y_send[0]] + [lax.ppermute(y_send[s], both, y_pairs(s)) for s in range(1, n_lon)]
    if not plan.apart:
        odd = lax.rem(lax.axis_index("lat"), 2) == 1
        ends = [jnp.concatenate([q[:, r].reshape(planes, sector), v[r]], axis=0) for r in (0, -1)]
        one = lax.ppermute(jnp.where(odd, ends[1], ends[0]), both, pairs_one)

    *x_send, to_one, first, last = pl.pallas_call(
        lambda *refs: travelling_kernel(plan, *refs),
        out_shape=[f32(plan.x_count, width)] * n_lon + [row_pair] + [f32(-(-rows // 8) * 8, plan.edge)] * 2,
        scratch_shapes=[vmem(n_lon, plan.x_count, width), *row_pads, vmem(plan.edge, LANES)],
        name="travel",
    )(q, u, v, two, two if plan.apart else one)
    x_got = [x_send[0]] + [lax.ppermute(x_send[s], both, x_pairs(s)) for s in range(1, n_lon)]
    if plan.apart:
        one = lax.ppermute(to_one, both, pairs_one)
    west = lax.ppermute(last, both, x_pairs(1))
    east = lax.ppermute(first, both, x_pairs(-1))

    out, sums = pl.pallas_call(
        lambda *refs: rest_kernel(plan, *refs),
        out_shape=[f32(fields, rows, levels, sector), f32(planes, LANES)],
        out_specs=[anywhere, whole],
        scratch_shapes=[*row_pads, vmem(fields, rows, levels, sector), vmem(LANES, plan.edge), pltpu.SemaphoreType.DMA],
        name="rest",
    )(q, u, v, one, two, west, east)

    tables = pl.pallas_call(
        lambda *refs: table_kernel(plan, *refs),
        out_shape=[pltpu.VMEM((2, size, size), jnp.bfloat16)] * 2
        + [pltpu.VMEM((2 * size, 2 * size), jnp.bfloat16)] * 2,
        name="tables",
    )()

    def filtered(got, count, rows_here, row_index, needed, pairs, name, *sums):
        ordered = [got[(n_lon - j) % n_lon] for j in range(n_lon)]
        pieces = pl.pallas_call(
            lambda *refs: filter_kernel(plan, count, rows_here, row_index, needed, bool(sums), *refs),
            out_shape=[f32(count, width)] * n_lon,
            in_specs=[smem] + [whole] * (4 + n_lon + len(sums)),
            name=name,
        )(cutoff, *tables, *ordered, *sums)
        return [pieces[0]] + [lax.ppermute(pieces[s], both, pairs(s)) for s in range(1, n_lon)]

    def placed(out, pieces, count, rows_here, row_index, needed, name, with_sums=False):
        return pl.pallas_call(
            lambda *refs: place_kernel(plan, count, rows_here, row_index, needed, with_sums, *refs),
            out_shape=f32(fields, rows, levels, sector),
            in_specs=[anywhere] + [whole] * n_lon,
            out_specs=anywhere,
            scratch_shapes=[
                vmem(n_lon, count, width),
                vmem(rows_here + with_sums, planes, sector),
                pltpu.SemaphoreType.DMA((rows_here + with_sums, fields)),
            ],
            input_output_aliases={0: 0},
            name=name,
        )(out, *pieces)

    def polar(lat):
        return plan.is_full(lat) | plan.is_part(lat)

    y_args = plan.y_count, plan.n_y, plan.y_row
    x_args = plan.x_count, plan.n_x, plan.x_row
    y_back = filtered(y_got, *y_args, plan.is_full, y_pairs, "filter_y")
    x_back = filtered(x_got, *x_args, polar, x_pairs, "filter_x", *([sums] if plan.apart else []))
    out = placed(out, y_back, *y_args, plan.is_full, "place_y")
    out = placed(out, x_back, *x_args, polar, "place_x", plan.apart)
    return jnp.transpose(out, (0, 2, 1, 3))


def solution(mesh):
    in_specs = (P(None, None, "lat", "lon"), P(None, "lat", "lon"), P(None, "lat", "lon"), P("lat"))
    out_specs = P(None, None, "lat", "lon")
    return jax.shard_map(body, mesh=mesh, in_specs=in_specs, out_specs=out_specs, check_vma=False)
```

```python
import math

import jax
import jax.numpy as jnp
from jax import lax
from jax.experimental import pallas as pl
from jax.experimental.pallas import tpu as pltpu
from jax.sharding import PartitionSpec as P


LANES = 128
EDGES = 5
FINE = 16
SUMS = 3
PARAMS = pltpu.CompilerParams(vmem_limit_bytes=24 * 2**20)


def padded(n):
    return -(-n // LANES) * LANES


class Plan:
    def __init__(self, fields, levels, rows, sector, n_lat, n_lon):
        self.fields, self.levels, self.rows, self.sector = fields, levels, rows, sector
        self.n_lat, self.n_lon = n_lat, n_lon
        self.planes = fields * levels
        self.circle = sector * n_lon
        self.quarter = self.circle // 4
        self.size = padded(self.quarter)
        cap = rows * n_lat // 6
        self.full = (cap - 1) // rows
        self.n_x = cap - self.full * rows
        self.apart = self.full == 1
        self.n_y = rows - self.n_x - self.apart
        self.width = padded(sector + EDGES)
        self.x_count = -(-self.n_x * self.planes // n_lon)
        self.y_count = -(-self.n_y * self.planes // (8 * n_lon)) * 8
        self.per_row = self.width // LANES
        self.x_rows = -(-(self.x_count + -(-rows // self.per_row)) // 8) * 8
        self.away = self.apart and n_lat >= 8 and n_lat % 4 == 0 and n_lon % 2 == 0
        self.x_full = list(range(1 + self.n_y, rows))
        if not self.apart:
            self.x_full = [0] + self.x_full
        self.edge = padded(self.planes + levels)
        self.sum_groups = -(-self.planes // self.x_count)

    def helper(self, south, lon):
        first, second = self.n_lat // 4, self.n_lat // 2
        if south:
            first, second = self.n_lat - 1 - first, self.n_lat - 1 - second
        return jnp.where(lon % 2 == 0, first, second) if isinstance(lon, jax.Array) else (first, second)[lon % 2]

    def filters_y(self, lat, lon):
        if not self.away:
            return self.is_full(lat)
        return (lat == self.helper(False, lon)) | (lat == self.helper(True, lon))

    def filters_x(self, lat, lon):
        return self.is_full(lat) | self.is_part(lat)

    def pieces(self, index, count):
        start, out = index * self.planes, []
        stop = start + self.planes
        while start < stop:
            chunk, offset = divmod(start, count)
            size = min(count - offset, stop - start)
            out.append((chunk, offset, start - index * self.planes, size))
            start += size
        return out

    def is_full(self, lat):
        return (lat < self.full) | (lat >= self.n_lat - self.full)

    def is_part(self, lat):
        return (lat == self.full) | (lat == self.n_lat - 1 - self.full)

    def x_row(self, index, lat):
        south = lat >= self.n_lat // 2
        partial = jnp.where(south, self.rows - self.n_x + index, index)
        full = jnp.where(south & self.apart, index, self.x_full[index])
        return jnp.where(self.is_full(lat), full, partial)

    def y_row(self, index, lat):
        south = lat >= self.n_lat // 2
        return jnp.where(south & self.apart, self.n_x + index, 1 + index)

    def pole_row(self, lat):
        return jnp.where(lat >= self.n_lat // 2, self.rows - 1, 0)


def split_speed(speed):
    return jnp.maximum(speed, 0.0), jnp.minimum(speed, 0.0)


def tiled(x, fields):
    return jnp.concatenate([x] * fields, axis=0) if fields > 1 else x


def back(x):
    return pltpu.roll(x, x.shape[1] - 1, 1)


def row_of(plan, q_ref, r):
    return q_ref[:, pl.ds(r, 1)].reshape(plan.planes, plan.sector)


def face_flux(plan, v_low, v_high, q_low, q_high):
    plus, minus = split_speed(0.5 * (v_low + v_high))
    return tiled(plus, plan.fields) * q_low + tiled(minus, plan.fields) * q_high


def emit(plan, buf, q_pad, u_pad, index, count, q_row, u_row, lat_divergence, cut):
    sector, fields = plan.sector, plan.fields
    q_pad[:, 0:sector] = q_row
    u_pad[:, 0:sector] = u_row
    q, u = q_pad[...], u_pad[...]
    inside = lax.broadcasted_iota(jnp.int32, u.shape, 1) < sector - 1
    plus, minus = split_speed(0.5 * (u + back(u)))
    plus, minus = jnp.where(inside, plus, 0.0), jnp.where(inside, minus, 0.0)
    east = tiled(plus, fields) * q + tiled(minus, fields) * back(q)
    q_pad[...] = q - (east - pltpu.roll(east, 1, 1))
    q_pad[:, 0:sector] = q_pad[:, 0:sector] - lat_divergence
    base = sector // LANES * LANES
    tail = q_pad[:, base:]
    lane = base + lax.broadcasted_iota(jnp.int32, tail.shape, 1)
    edges = q[:, 0:1], q[:, sector - 1 : sector], u[:, 0:1], u[:, sector - 1 : sector]
    for k, value in enumerate(edges):
        tail = jnp.where(lane == sector + k, value if k < 2 else tiled(value, fields), tail)
    q_pad[:, base:] = jnp.where(lane == sector + 4, cut.astype(jnp.float32), tail)
    for chunk, offset, start, size in plan.pieces(index, count):
        buf[chunk, offset : offset + size, :] = q_pad[start : start + size, :]


def hand_out(plan, buf, outs):
    lon = lax.axis_index("lon")
    for s in range(plan.n_lon):
        outs[s][...] = buf[lax.rem(lon + s, plan.n_lon)]


def inner_kernel(plan, cut_ref, q_ref, u_ref, v_ref, *refs):
    outs, (two, one, buf, q_pad, u_pad) = refs[: plan.n_lon], refs[plan.n_lon :]
    planes, rows = plan.planes, plan.rows
    lat = lax.axis_index("lat")
    q_pad[...] = jnp.zeros_like(q_pad)
    u_pad[...] = jnp.zeros_like(u_pad)
    first = plan.y_row(0, lat)

    def south_flux(r):
        return face_flux(plan, v_ref[r], v_ref[r + 1], row_of(plan, q_ref, r), row_of(plan, q_ref, r + 1))

    north = south_flux(first - 1)
    for i in range(plan.n_y):
        r = first + i
        south = south_flux(r)
        emit(plan, buf, q_pad, u_pad, i, plan.y_count, row_of(plan, q_ref, r), u_ref[r], south - north, cut_ref[r])
        north = south
    hand_out(plan, buf, outs)
    for out, odd, even in ((two, 0, rows - 1), (one, rows - 1, 0)):
        r = jnp.where(lax.rem(lat, 2) == 1, odd, even)
        out[0:planes, :] = row_of(plan, q_ref, r)
        out[planes:, :] = v_ref[r]


def ghosts(plan, one_ref, two_ref):
    lat = lax.axis_index("lat")
    odd = lax.rem(lat, 2) == 1
    sign_north = jnp.where(lat == 0, -1.0, 1.0)
    sign_south = jnp.where(lat == plan.n_lat - 1, -1.0, 1.0)
    one, two, planes = one_ref[...], two_ref[...], plan.planes
    above, below = jnp.where(odd, two, one), jnp.where(odd, one, two)
    return above[:planes], above[planes:] * sign_north, below[:planes], below[planes:] * sign_south


def lat_divergence(plan, q_ref, v_ref, r, around):
    q_above, v_above, q_below, v_below = around
    rows = plan.rows
    before, after = jnp.maximum(r - 1, 0), jnp.minimum(r + 1, rows - 1)
    top, bottom = r == 0, r == rows - 1
    q_row, v_row = row_of(plan, q_ref, r), v_ref[r]
    v_south = jnp.where(bottom, v_below, v_ref[after])
    q_south = jnp.where(bottom, q_below, row_of(plan, q_ref, after))
    v_north = jnp.where(top, v_above, v_ref[before])
    q_north = jnp.where(top, q_above, row_of(plan, q_ref, before))
    south = face_flux(plan, v_row, v_south, q_row, q_south)
    return south - face_flux(plan, v_north, v_row, q_north, q_row)


def travelling_kernel(plan, cut_ref, q_ref, u_ref, v_ref, two_ref, one_ref, *refs):
    n = plan.n_lon
    outs, (buf, q_pad, u_pad, columns) = refs[:n], refs[n:]
    planes, sector, rows = plan.planes, plan.sector, plan.rows
    lat = lax.axis_index("lat")
    around = ghosts(plan, one_ref, two_ref)
    q_pad[...] = jnp.zeros_like(q_pad)
    u_pad[...] = jnp.zeros_like(u_pad)
    for j in range(plan.n_x):
        r = plan.x_row(j, lat)
        divergence = lat_divergence(plan, q_ref, v_ref, r, around)
        emit(plan, buf, q_pad, u_pad, j, plan.x_count, row_of(plan, q_ref, r), u_ref[r], divergence, cut_ref[r])
    hand_out(plan, buf, outs)
    columns[...] = jnp.zeros_like(columns)
    for out, at in ((outs[n - 1], 0), (outs[1], sector - 1)):
        for r in range(rows):
            columns[0:planes, r : r + 1] = row_of(plan, q_ref, r)[:, at : at + 1]
            columns[planes : planes + plan.levels, r : r + 1] = u_ref[r][:, at : at + 1]
        flat = columns[...].T
        for r in range(rows):
            row, lane = plan.x_count + r // plan.per_row, r % plan.per_row * LANES
            out[row : row + 1, lane : lane + plan.edge] = flat[r : r + 1]


def lon_step(plan, q_pad, u_pad, q_row, u_row, east_column, west_column):
    sector, width, planes = plan.sector, plan.width, plan.planes
    q_pad[:, 0:sector] = q_row
    u_pad[:, 0:sector] = u_row
    q_pad[:, sector : sector + 1] = east_column[:planes]
    u_pad[:, sector : sector + 1] = east_column[planes : planes + plan.levels]
    q_pad[:, width - 1 : width] = west_column[:planes]
    u_pad[:, width - 1 : width] = west_column[planes : planes + plan.levels]
    q, u = q_pad[...], u_pad[...]
    plus, minus = split_speed(0.5 * (u + back(u)))
    east = tiled(plus, plan.fields) * q + tiled(minus, plan.fields) * back(q)
    return q - (east - pltpu.roll(east, 1, 1))


def sector_turns(plan, shape):
    at = lax.axis_index("lon") * plan.sector + lax.broadcasted_iota(jnp.int32, shape, 1)
    return turn(at.astype(jnp.float32), plan.circle)


def columns_of(plan, ref, pack):
    pack[...] = jnp.zeros_like(pack)
    for r in range(plan.rows):
        row, lane = plan.x_count + r // plan.per_row, r % plan.per_row * LANES
        pack[r : r + 1, :] = ref[row : row + 1, lane : lane + plan.edge]
    return pack[...].T


def rest_kernel(plan, q_ref, u_ref, v_ref, one_ref, two_ref, west_ref, east_ref, out, q_pad, u_pad, stage, pack, sem):
    sector, rows = plan.sector, plan.rows

    @pl.when(jnp.logical_not(plan.is_full(lax.axis_index("lat"))))
    def _():
        q_above, v_above, q_below, v_below = ghosts(plan, one_ref, two_ref)
        q_pad[...] = jnp.zeros_like(q_pad)
        u_pad[...] = jnp.zeros_like(u_pad)
        east_columns = columns_of(plan, east_ref, pack)
        west_columns = columns_of(plan, west_ref, pack)
        north = face_flux(plan, v_above, v_ref[0], q_above, row_of(plan, q_ref, 0))
        for r in range(rows):
            q_row = row_of(plan, q_ref, r)
            stepped = lon_step(
                plan, q_pad, u_pad, q_row, u_ref[r], east_columns[:, r : r + 1], west_columns[:, r : r + 1]
            )
            inner = r + 1 < rows
            south = face_flux(
                plan,
                v_ref[r],
                v_ref[r + 1] if inner else v_below,
                q_row,
                row_of(plan, q_ref, r + 1) if inner else q_below,
            )
            value = stepped[:, 0:sector] - (south - north)
            stage[:, r : r + 1] = value.reshape(plan.fields, 1, plan.levels, sector)
            north = south
        copy = pltpu.make_async_copy(stage, out, sem)
        copy.start()
        copy.wait()


def pole_kernel(plan, q_ref, u_ref, v_ref, one_ref, two_ref, west_ref, east_ref, sums, q_pad, u_pad, pack):
    lat = lax.axis_index("lat")

    @pl.when(plan.is_full(lat))
    def _():
        q_pad[...] = jnp.zeros_like(q_pad)
        u_pad[...] = jnp.zeros_like(u_pad)
        r = plan.pole_row(lat)
        lane = lax.broadcasted_iota(jnp.int32, (plan.edge, LANES), 1)

        def column(ref):
            return jnp.sum(jnp.where(lane == r, columns_of(plan, ref, pack), 0.0), axis=1, keepdims=True)

        stepped = lon_step(plan, q_pad, u_pad, row_of(plan, q_ref, r), u_ref[r], column(east_ref), column(west_ref))
        around = ghosts(plan, one_ref, two_ref)
        value = stepped[:, 0 : plan.sector] - lat_divergence(plan, q_ref, v_ref, r, around)
        cos, sin = sector_turns(plan, (1, plan.sector))
        for k, part in enumerate((value, value * cos, value * sin)):
            sums[:, k : k + 1] = jnp.sum(part, axis=1, keepdims=True)


def turn(numerator, circle):
    p = numerator - circle * jnp.floor(numerator * (1.0 / circle))
    j = jnp.floor(p * (4.0 / circle) + 0.5)
    x = (p - j * (circle / 4)) * (2.0 * math.pi / circle)
    z = x * x
    s = x * (1 + z * (-1 / 6 + z * (1 / 120 + z * (-1 / 5040 + z * (1 / 362880)))))
    c = 1 + z * (-1 / 2 + z * (1 / 24 + z * (-1 / 720 + z * (1 / 40320 + z * (-1 / 3628800)))))
    swap = (j == 1.0) | (j == 3.0)
    cos, sin = jnp.where(swap, s, c), jnp.where(swap, c, s)
    cos = jnp.where((j == 1.0) | (j == 2.0), -cos, cos)
    sin = jnp.where((j == 2.0) | (j == 3.0), -sin, sin)
    return cos, sin


def table_kernel(plan, even_hi, even_lo, odd_hi, odd_lo):
    size = plan.size
    coarse = size // FINE

    def numerators(count, step, r):
        n = step * lax.broadcasted_iota(jnp.int32, (count, size), 0)
        k = 4 * lax.broadcasted_iota(jnp.int32, (count, size), 1) + r
        return (n * k).astype(jnp.float32)

    def put(hi, lo, index, value):
        high = value.astype(jnp.bfloat16)
        hi[index] = high
        lo[index] = (value - high.astype(jnp.float32)).astype(jnp.bfloat16)

    for r in range(4):
        cos_c, sin_c = turn(numerators(coarse, FINE, r), plan.circle)
        cos_f, sin_f = turn(numerators(FINE, 1, r), plan.circle)
        sum_f, gap_f = cos_f + sin_f, cos_f - sin_f
        column = slice(0, size) if r < 2 else slice(size, 2 * size)
        for i in range(coarse):
            c, s = cos_c[i : i + 1], sin_c[i : i + 1]
            rows = slice(i * FINE, (i + 1) * FINE)
            plus = c * sum_f + s * gap_f
            if r % 2 == 0:
                put(even_hi, even_lo, (r // 2, rows), plus)
            else:
                minus = c * gap_f - s * sum_f
                put(odd_hi, odd_lo, (rows, column), plus)
                rows = slice(size + i * FINE, size + (i + 1) * FINE)
                put(odd_hi, odd_lo, (rows, column), minus if r == 1 else -minus)


def product(x, table_hi, table_lo, transposed):
    dims = (((1,), (1 if transposed else 0,)), ((), ()))
    x_hi = x.astype(jnp.bfloat16)
    count, wide = x.shape[0], x_hi.astype(jnp.float32)
    halves = jnp.concatenate([wide, x - wide], axis=0).astype(jnp.bfloat16)
    both = lax.dot_general(halves, table_hi, dims, preferred_element_type=jnp.float32)
    low = lax.dot_general(x_hi, table_lo, dims, preferred_element_type=jnp.float32)
    return both[:count] + both[count:] + low


def filter_quarters(plan, quarters, cut, even_hi, even_lo, odd_hi, odd_lo):
    x0, x1, x2, x3 = quarters
    size, circle = plan.size, plan.circle
    a, b, odd = x0 + x2, x1 + x3, jnp.concatenate([x0 - x2, x1 - x3], axis=1)

    def kept(h, k, m):
        ok = (jnp.minimum(k, circle - k).astype(jnp.float32) <= cut) & (m < plan.quarter)
        return jnp.where(ok, h, 0.0) * (1.0 / circle)

    m = lax.broadcasted_iota(jnp.int32, x0.shape, 1)
    lane = lax.broadcasted_iota(jnp.int32, odd.shape, 1)
    m_odd = jnp.where(lane < size, lane, lane - size)
    k_odd = 4 * m_odd + jnp.where(lane < size, 1, 3)
    tables = [(even_hi[0], even_lo[0]), (even_hi[1], even_lo[1]), (odd_hi[...], odd_lo[...])]
    h0 = kept(product(a + b, *tables[0], False), 4 * m, m)
    h2 = kept(product(a - b, *tables[1], False), 4 * m + 2, m)
    h13 = kept(product(odd, *tables[2], False), k_odd, m_odd)
    even, twice = product(h0, *tables[0], True), product(h2, *tables[1], True)
    other = product(h13, *tables[2], True)
    both, apart = even + twice, even - twice
    o_u, o_v = other[:, :size], other[:, size:]
    return both + o_u, apart + o_v, both - o_u, apart - o_v


def filter_kernel(plan, needed, with_sums, *refs):
    n = plan.n_lon
    tables, ins, outs = refs[:4], refs[4 : 4 + n], refs[-n:]
    sector, width, count = plan.sector, plan.width, ins[0].shape[0]

    @pl.when(needed(lax.axis_index("lat"), lax.axis_index("lon")))
    def _():
        cut = ins[0][:, sector + 4 : sector + 5]
        lane = lax.broadcasted_iota(jnp.int32, (count, width), 1)
        pieces = [jnp.where(lane < sector, ref[...], 0.0) for ref in ins]
        tails = [ref[:, sector : sector + EDGES] for ref in ins]
        fluxes = []
        for j in range(n):
            here, there = tails[j], tails[(j + 1) % n]
            plus, minus = split_speed(0.5 * (here[:, 3:4] + there[:, 2:3]))
            fluxes.append(plus * here[:, 1:2] + minus * there[:, 0:1])
        pieces = [
            piece
            - jnp.where(lane == sector - 1, fluxes[j], 0.0)
            + jnp.where(lane == 0, fluxes[j - 1], 0.0)
            for j, piece in enumerate(pieces)
        ]
        per = n // 4
        if per == 1 and width == plan.size:
            quarters = pieces
        else:
            spare = [jnp.zeros((count, plan.size - plan.quarter), jnp.float32)] * (plan.size > plan.quarter)
            quarters = [
                jnp.concatenate([p[:, :sector] for p in pieces[per * i : per * (i + 1)]] + spare, axis=1)
                for i in range(4)
            ]
        filtered = filter_quarters(plan, quarters, cut, *tables)
        for j in range(n):
            part = j % per
            outs[j][:, 0:sector] = filtered[j // per][:, part * sector : (part + 1) * sector]
        if with_sums:
            sums = refs[4 + n]
            for g in range(plan.sum_groups):
                start = g * plan.x_count
                size = min(plan.x_count, plan.planes - start)
                at = sector + SUMS * g
                for j in range(n):
                    outs[j][0:size, at : at + SUMS] = sums[start : start + size, 0:SUMS]


def place_kernel(plan, count, rows_here, row_index, needed, with_sums, whole, *refs):
    n = plan.n_lon
    ins, (out, buf, row_buf, sems) = refs[:n], refs[n:]
    lat, lon = lax.axis_index("lat"), lax.axis_index("lon")

    def copies(i, row):
        return [
            pltpu.make_async_copy(
                row_buf.at[i, pl.ds(f * plan.levels, plan.levels)], out.at[f, row], sems.at[i, f]
            )
            for f in range(plan.fields)
        ]

    def start(i, row):
        for copy in copies(i, row):
            copy.start()

    def wait(i, row):
        for copy in copies(i, row):
            copy.wait()

    @pl.when(needed(lat, lon))
    def _():
        for j in range(n):
            buf[lax.rem(lon + n - j, n)] = ins[j][...]
        for i in range(rows_here):
            for chunk, offset, first, size in plan.pieces(i, count):
                row_buf[i, first : first + size, :] = buf[chunk, offset : offset + size, 0 : plan.sector]
            start(i, row_index(i, lat))

    if with_sums:

        @pl.when(plan.is_full(lat))
        def _():
            i = rows_here
            cos, sin = sector_turns(plan, (1, plan.sector))
            for g in range(plan.sum_groups):
                size = min(count, plan.planes - g * count)
                at = plan.sector + SUMS * g
                total = sum(ref[0:size, at : at + SUMS] for ref in ins)
                row_buf[i, g * count : g * count + size, :] = (
                    total[:, 0:1] + 2.0 * (total[:, 1:2] * cos + total[:, 2:3] * sin)
                ) * (1.0 / plan.circle)
            start(i, plan.pole_row(lat))
            wait(i, plan.pole_row(lat))

    @pl.when(needed(lat, lon))
    def _():
        for i in range(rows_here):
            wait(i, row_index(i, lat))


def f32(*shape):
    return jax.ShapeDtypeStruct(shape, jnp.float32)


def vmem(*shape):
    return pltpu.VMEM(shape, jnp.float32)


def on_chip(x):
    return pltpu.with_memory_space_constraint(x, pltpu.VMEM)


def off_chip(x):
    return pltpu.with_memory_space_constraint(x, pltpu.HBM)


def body(tracers, zonal_wind, meridional_wind, cutoff):
    fields, levels, rows, sector = tracers.shape
    n_lat, n_lon = lax.axis_size("lat"), lax.axis_size("lon")
    plan = Plan(fields, levels, rows, sector, n_lat, n_lon)
    planes, width, size = plan.planes, plan.width, plan.size
    q = jnp.transpose(tracers, (0, 2, 1, 3))
    u, v = (jnp.transpose(x, (1, 0, 2)) for x in (zonal_wind, meridional_wind))

    def permuted(x, pairs):
        return on_chip(lax.ppermute(x, ("lat", "lon"), pairs))

    def device(lat, lon):
        return lat * n_lon + lon % n_lon

    def shift_pairs(lats, by):
        return [(device(a, z), device(a, z + by)) for a in lats for z in range(n_lon)]

    def x_pairs(by):
        return shift_pairs(range(n_lat), by)

    def x_back_pairs(by):
        if not plan.away:
            return x_pairs(by)
        polar = [0, 1, n_lat - 2, n_lat - 1]
        pairs = shift_pairs(polar, by)
        for a in range(2, n_lat - 2, 2):
            pairs += swapped(a, a + 1)
        return pairs

    def swapped(a, b):
        return [(device(p, z), device(q, z)) for p, q in ((a, b), (b, a)) for z in range(n_lon)]

    def beside(lat_sets, fill):
        pairs = []
        for z in range(n_lon):
            used = {0, n_lat - 1, plan.helper(False, z), plan.helper(True, z)}
            other = ((1, plan.helper(False, z + 1)), (n_lat - 2, plan.helper(True, z + 1)))
            used.update(a for pair in other for a in pair)
            free = [a for a in range(n_lat) if a not in used]
            for a, b in other + tuple(zip(free[0::2], free[1::2])):
                pairs += [(device(a, z), device(b, z)), (device(b, z), device(a, z))]
            for pole, south in ((0, False), (n_lat - 1, True)):
                pairs += [(device(pole, z), device(plan.helper(south, lat_sets(z)), lat_sets(z)))]
                pairs += [(device(plan.helper(south, z), z), device(pole, fill(z)))]
        return pairs

    def y_pairs(by):
        if plan.away:
            return beside(lambda z: (z + by) % n_lon, lambda z: (z - by) % n_lon)
        spare = list(range(plan.full + 1, n_lat - plan.full - 1))
        pairs = shift_pairs(list(range(plan.full)) + list(range(n_lat - plan.full, n_lat)), by)
        pairs += swapped(plan.full, n_lat - 1 - plan.full)
        for a, b in zip(spare[0::2], spare[1::2]):
            pairs += swapped(a, b)
        return pairs

    def y_back_pairs(by):
        return beside(lambda z: z, lambda z: (z + by) % n_lon) if plan.away else y_pairs(by)

    pairs_one = shift_pairs((0, n_lat - 1), n_lon // 2)
    for a in range(1, n_lat - 1, 2):
        pairs_one += swapped(a, a + 1)
    pairs_two = [pair for a in range(0, n_lat, 2) for pair in swapped(a, a + 1)]

    whole = pl.BlockSpec(memory_space=pltpu.VMEM)
    smem = pl.BlockSpec(memory_space=pltpu.SMEM)
    anywhere = pl.BlockSpec(memory_space=pl.ANY)
    row_pads = [vmem(planes, width), vmem(levels, width)]
    row_pair = vmem(planes + levels, sector)

    *y_send, to_two, to_one = pl.pallas_call(
        lambda *refs: inner_kernel(plan, *refs),
        out_shape=[vmem(plan.y_count, width)] * n_lon + [row_pair] * 2,
        in_specs=[smem] + [whole] * 3,
        scratch_shapes=[vmem(n_lon, plan.y_count, width), *row_pads],
        compiler_params=PARAMS,
        name="inner",
    )(off_chip(cutoff), off_chip(q), off_chip(u), off_chip(v))
    two = permuted(to_two, pairs_two)
    y_kept = [] if plan.away else [on_chip(y_send[0])]
    y_got = y_kept + [permuted(y_send[s], y_pairs(s)) for s in range(len(y_kept), n_lon)]
    one = permuted(to_one, pairs_one)

    x_send = pl.pallas_call(
        lambda *refs: travelling_kernel(plan, *refs),
        out_shape=[vmem(plan.x_rows, width)] * n_lon,
        in_specs=[smem] + [whole] * 5,
        scratch_shapes=[vmem(n_lon, plan.x_rows, width), *row_pads, vmem(plan.edge, LANES)],
        compiler_params=PARAMS,
        name="travel",
    )(cutoff, q, u, v, two, two if plan.apart else one)
    x_got = [on_chip(x_send[0])] + [permuted(x_send[s], x_pairs(s)) for s in range(1, n_lon)]
    west, east = x_got[1], x_got[n_lon - 1]

    out = pl.pallas_call(
        lambda *refs: rest_kernel(plan, *refs),
        out_shape=f32(fields, rows, levels, sector),
        out_specs=anywhere,
        scratch_shapes=[*row_pads, vmem(fields, rows, levels, sector), vmem(LANES, plan.edge), pltpu.SemaphoreType.DMA],
        compiler_params=PARAMS,
        name="rest",
    )
    out = out(q, u, v, one, two, west, east)
    sums = []
    if plan.apart:
        sums = [
            on_chip(
                pl.pallas_call(
                    lambda *refs: pole_kernel(plan, *refs),
                    out_shape=vmem(planes, LANES),
                    scratch_shapes=[*row_pads, vmem(LANES, plan.edge)],
                    compiler_params=PARAMS,
                    name="pole",
                )(q, u, v, one, two, west, east)
            )
        ]

    make_tables = pl.pallas_call(
        lambda *refs: table_kernel(plan, *refs),
        out_shape=[pltpu.VMEM((2, size, size), jnp.bfloat16)] * 2
        + [pltpu.VMEM((2 * size, 2 * size), jnp.bfloat16)] * 2,
        compiler_params=PARAMS,
        name="tables",
    )
    tables = make_tables()
    tables = [on_chip(table) for table in tables]

    def filtered(got, needed, pairs, first, *sums):
        ordered = [got[(n_lon - j) % n_lon] for j in range(n_lon)]
        call = pl.pallas_call(
            lambda *refs: filter_kernel(plan, needed, bool(sums), *refs),
            out_shape=[vmem(*got[0].shape)] * n_lon,
            in_specs=[whole] * (4 + n_lon + len(sums)),
            compiler_params=PARAMS,
        )
        pieces = call(*tables, *ordered, *sums)
        kept = [on_chip(piece) for piece in pieces[:first]]
        return kept + [permuted(pieces[s], pairs(s)) for s in range(first, n_lon)]

    def placed(out, pieces, count, rows_here, row_index, needed, with_sums=False):
        return pl.pallas_call(
            lambda *refs: place_kernel(plan, count, rows_here, row_index, needed, with_sums, *refs),
            out_shape=f32(fields, rows, levels, sector),
            in_specs=[anywhere] + [whole] * n_lon,
            out_specs=anywhere,
            scratch_shapes=[
                vmem(n_lon, *pieces[0].shape),
                vmem(rows_here + with_sums, planes, sector),
                pltpu.SemaphoreType.DMA((rows_here + with_sums, fields)),
            ],
            input_output_aliases={0: 0},
            compiler_params=PARAMS,
        )(out, *pieces)

    x_back = filtered(x_got, plan.filters_x, x_back_pairs, 1, *sums)
    y_back = filtered(y_got, plan.filters_y, y_back_pairs, len(y_kept))

    def full(lat, lon):
        return plan.is_full(lat)

    out = placed(out, y_back, plan.y_count, plan.n_y, plan.y_row, full)
    out = placed(out, x_back, plan.x_count, plan.n_x, plan.x_row, plan.filters_x, plan.apart)
    return jnp.transpose(out, (0, 2, 1, 3))


def solution(mesh):
    in_specs = (P(None, None, "lat", "lon"), P(None, "lat", "lon"), P(None, "lat", "lon"), P("lat"))
    out_specs = P(None, None, "lat", "lon")

    return jax.shard_map(body, mesh=mesh, in_specs=in_specs, out_specs=out_specs, check_vma=False)
```
